512 devices in a mesh: dp: 16 (over z, core), fsdp: 32 (over y, x).
Axes of the slice: x: 4, y: 8, z: 8, core: 2. Of those that a mesh axis runs over, the one named last changes fastest.
Arguments:
- out_grad: bfloat16 [4096, 4096], P(('dp', 'fsdp')), may hold values from -6 to 6
- gate_pre: bfloat16 [4096, 14848], P('dp', 'fsdp'), may hold values from -6 to 6
- up_pre: bfloat16 [4096, 14848], P('dp', 'fsdp'), may hold values from -6 to 6
- down_weight: bfloat16 [14848, 4096], P('fsdp', 'dp'), may hold values from -0.09375 to 0.09375
- momentum: float32 [16, 14848, 256], P('dp', 'fsdp'), may hold values from -6 to 6
- band_index: int32 [16, 14848, 32], P('dp', 'fsdp'), may hold values from 0 to 255, as said below
- band_count: int32 [16, 14848], P('dp', 'fsdp'), may hold values from 1 to 32, as said below
Outputs:
- gate_grad: bfloat16 [4096, 14848], P('dp', 'fsdp')
- up_grad: bfloat16 [4096, 14848], P('dp', 'fsdp')
- new_momentum: float32 [16, 14848, 256], P('dp', 'fsdp')
- update: float32 [14848, 256], P('fsdp')
The draws below stay inside these ranges and needn't reach their ends.
Inputs may be any that keep to these rules, and one draw needn't show every extreme that they name: `band_index`: for each worker and block the 32 entries of the list are different frequencies. `band_count`: on every worker some block uses all 32 entries and some block uses one.
All inputs are finite; a program needn't handle non-finite values.
Results may differ from the reference program's by a relative error of at most 0.0019.
Values may be sent and summed in bfloat16 or wider, within the bound.
No kernel may reach another device: no remote copies, remote signals or barrier semaphores. Data moves between devices by JAX's collectives and lax.ppermute only.
A program may use at most 64 MiB of HBM per device.

```python
import math
import jax
import jax.numpy as jnp
from jax import lax

HIDDEN_SIZE = 14848
FEATURES = 4096
COLUMNS = 256
BLOCK_LEN = 256
BAND_SLOTS = 32
TOK_WORKER = 256
TOKENS = 4096
BLOCKS = 14848
N_DP = 16


def draw_band_index(key, part):
    scores = jax.random.randint(key, (N_DP, BLOCKS, BLOCK_LEN), 0, 1 << 20)
    scores = scores * BLOCK_LEN + jnp.arange(BLOCK_LEN, dtype=jnp.int32)[None, None, :]
    ordering = jnp.argsort(scores, axis=2)
    return ordering[:, :, :BAND_SLOTS].astype(jnp.int32)


def draw_band_count(key, part):
    split_keys = jax.random.split(jax.random.fold_in(key, 17), 4)
    ranking = jax.random.permutation(split_keys[0], N_DP).astype(jnp.int32)
    lowest = 1 + ranking * (BAND_SLOTS - 1) // N_DP
    spread = BAND_SLOTS + 1 - lowest
    raw_draw = jax.random.randint(split_keys[1], (N_DP, BLOCKS), 0, 1 << 20)
    counts = raw_draw % spread[:, None] + lowest[:, None]
    full_at = jax.random.randint(split_keys[2], (N_DP,), 0, BLOCKS)
    one_at = (full_at + 1 + jax.random.randint(split_keys[3], (N_DP,), 0, BLOCKS - 1)) % BLOCKS
    positions = jnp.arange(BLOCKS, dtype=jnp.int32)[None, :]
    counts = jnp.where(positions == full_at[:, None], BAND_SLOTS, counts)
    counts = jnp.where(positions == one_at[:, None], 1, counts)
    return counts.astype(jnp.int32)


def block_levels(own_key, shape, pieces, smallest, high):
    def one(dim, blocks):
        steps = jax.random.uniform(jax.random.fold_in(jax.random.fold_in(own_key, 6), dim), (blocks,), jnp.float32, smallest / len(pieces), high / len(pieces))
        return jnp.repeat(jnp.exp(steps), shape[dim] // blocks).reshape((-1,) + (1,) * (len(shape) - dim - 1))

    gain = one(*pieces[0])
    for cut in pieces[1:]:
        gain = gain * one(*cut)
    return gain


def centred(rng, extent, deviation, bound, cuts=(), kind=jnp.bfloat16):
    factor_of = block_levels(rng, extent, cuts, -0.22, 0.18) if cuts else 1.0
    drawn = jax.random.normal(rng, extent, jnp.float32) * deviation * factor_of
    return jnp.minimum(jnp.maximum(drawn, -bound), bound).astype(kind)


def setup_inputs(seed: int = 0) -> dict:
    seeds = jax.random.split(jax.random.key(seed), 8)
    out_grad = centred(seeds[0], (TOKENS, FEATURES), 1.0, 6.0, ((0, 512),))
    gate_pre = centred(seeds[1], (TOKENS, HIDDEN_SIZE), 1.0, 6.0, ((0, 16), (1, 32)))
    up_pre = centred(seeds[2], (TOKENS, HIDDEN_SIZE), 1.0, 6.0, ((0, 16), (1, 32)))
    down_weight = centred(seeds[3], (HIDDEN_SIZE, FEATURES), FEATURES ** -0.5, 0.09375, ((0, 32), (1, 16)))
    momentum = centred(seeds[4], (N_DP, HIDDEN_SIZE, COLUMNS), 1.0, 6.0, ((0, 16), (1, 32)), jnp.float32)
    band_index = draw_band_index(jax.random.fold_in(seeds[7], 71), 0)
    band_count = draw_band_count(jax.random.fold_in(seeds[7], 71), 0)
    return {"out_grad": out_grad, "gate_pre": gate_pre, "up_pre": up_pre, "down_weight": down_weight, "momentum": momentum, "band_index": band_index, "band_count": band_count}


momentum_decay = 0.9

def cosine_matrix(length):
    frequency = jnp.arange(length, dtype=jnp.int32).astype(jnp.float32)[:, None]
    position = jnp.arange(length, dtype=jnp.int32).astype(jnp.float32)[None, :]
    angles = math.pi * (position + 0.5) * frequency / length
    row_weight = jnp.where(frequency == 0.0, math.sqrt(1.0 / length), math.sqrt(2.0 / length))
    return jnp.cos(angles) * row_weight

def reference(out_grad, gate_pre, up_pre, down_weight, momentum, band_index, band_count):
    gate_float = gate_pre.astype(jnp.float32)
    up_float = up_pre.astype(jnp.float32)
    sigmoid_gate = jax.nn.sigmoid(gate_float)
    activation = gate_float * sigmoid_gate
    hidden = (activation * up_float).astype(jnp.bfloat16)
    hidden_grad = jnp.dot(out_grad, down_weight.T, preferred_element_type=jnp.float32)
    up_grad = (hidden_grad * activation).astype(jnp.bfloat16)
    gate_grad = (hidden_grad * up_float * sigmoid_gate * (1.0 + gate_float * (1.0 - sigmoid_gate))).astype(jnp.bfloat16)
    grad_scale = 1.0 / math.sqrt(TOK_WORKER)
    hidden_workers = hidden.reshape(N_DP, TOK_WORKER, HIDDEN_SIZE)
    window_workers = out_grad[:, :COLUMNS].reshape(N_DP, TOK_WORKER, COLUMNS)

    def worker_grad(member_pair):
        return jnp.dot(member_pair[0].T, member_pair[1], preferred_element_type=jnp.float32) * grad_scale
    worker_grads = lax.map(worker_grad, (hidden_workers, window_workers))
    cosine_table = cosine_matrix(BLOCK_LEN)
    mixed = momentum_decay * momentum + worker_grads
    blocked = mixed.reshape(N_DP, BLOCKS, BLOCK_LEN)
    frequency = jnp.arange(BLOCK_LEN, dtype=jnp.int32)
    slot_ids = jnp.arange(BAND_SLOTS, dtype=jnp.int32)

    def one_worker(member):
        rows_blocked, slot_list, counts = member
        spectrum = jnp.dot(rows_blocked, cosine_table.T, precision=lax.Precision.HIGHEST)
        picked = jnp.take_along_axis(spectrum, slot_list, axis=1)
        band_values = jnp.where(slot_ids[None, :] < counts[:, None], picked, 0.0)
        own_spectrum = lax.optimization_barrier(jnp.sum(jnp.where(slot_list[:, :, None] == frequency[None, None, :], band_values[:, :, None], 0.0), axis=1))
        momentum_kept = rows_blocked - jnp.dot(own_spectrum, cosine_table, precision=lax.Precision.HIGHEST)
        return (momentum_kept, own_spectrum)
    kept_all, sent_all = lax.map(one_worker, (blocked, band_index, band_count))
    averaged = lax.optimization_barrier(jnp.sum(sent_all, axis=0)) / N_DP
    update = jnp.dot(averaged, cosine_table, precision=lax.Precision.HIGHEST).reshape(HIDDEN_SIZE, COLUMNS)
    new_momentum = kept_all.reshape(N_DP, HIDDEN_SIZE, COLUMNS)
    return (gate_grad, up_grad, new_momentum, update)
```

```python
import functools
import math

import jax
import jax.numpy as jnp
from jax import lax
from jax.experimental import pallas as pl
from jax.experimental.pallas import tpu as pltpu
from jax.sharding import Mesh
from jax.sharding import PartitionSpec as P

DP = ("z", "core")
FSDP = ("y", "x")
momentum_decay = 0.9


def cosine_matrix(length):
    frequency = jnp.arange(length, dtype=jnp.int32).astype(jnp.float32)[:, None]
    position = jnp.arange(length, dtype=jnp.int32).astype(jnp.float32)[None, :]
    angles = math.pi * (position + 0.5) * frequency / length
    row_weight = jnp.where(frequency == 0.0, math.sqrt(1.0 / length), math.sqrt(2.0 / length))
    return jnp.cos(angles) * row_weight


def gathered(value, axis):
    count = lax.axis_size(axis)
    copies = jnp.broadcast_to(value[None], (count, *value.shape))
    return lax.all_to_all(copies, axis, 0, 0)


def gathered_over_y(value):
    me = lax.axis_index("y")
    even = me % 2 == 0
    blocks = jnp.zeros((8, *value.shape), value.dtype)

    def put(blocks, piece, at):
        return lax.dynamic_update_slice(blocks, piece, (at, 0, 0))

    blocks = put(blocks, value[None], me)
    got = lax.ppermute(value, "y", [(i, i ^ 1) for i in range(8)])
    blocks = put(blocks, got[None], me ^ 1)
    own_pair = me // 2
    pair = jnp.where(even, jnp.stack([value, got]), jnp.stack([got, value]))
    second = [(i, (i - 1) % 8 if i % 2 == 0 else (i + 1) % 8) for i in range(8)]
    got_pair = lax.ppermute(pair, "y", second)
    next_pair = jnp.where(even, own_pair + 3, own_pair + 1) % 4
    blocks = put(blocks, got_pair, next_pair * 2)
    third = [(i, (i + 3) % 8 if i % 2 == 0 else (i - 3) % 8) for i in range(8)]
    got_four = lax.ppermute(jnp.concatenate([pair, got_pair]), "y", third)
    far = jnp.where(even, me + 3, me + 5) % 8
    far_pair = far // 2
    far_next = jnp.where(even, far_pair + 1, far_pair + 3) % 4
    blocks = put(blocks, got_four[:2], far_pair * 2)
    return put(blocks, got_four[2:], far_next * 2)


def gathered_over_x(value):
    me = lax.axis_index("x")
    whole = jnp.zeros((value.shape[0], 4, *value.shape[1:]), value.dtype)
    pieces = [value] + [
        lax.ppermute(value, "x", [(i, (i + s) % 4) for i in range(4)]) for s in (1, 3, 2)
    ]
    for piece, s in zip(pieces, (0, 1, 3, 2)):
        whole = lax.dynamic_update_slice(whole, piece[:, None], (0, (me + 4 - s) % 4, 0, 0))
    return whole


def product_kernel(grad_ref, weight_ref, gate_ref, up_ref, gate_grad_ref, up_grad_ref, total_ref):
    step = pl.program_id(0)

    @pl.when(step == 0)
    def _():
        total_ref[...] = jnp.zeros_like(total_ref)

    width = weight_ref.shape[2]
    for b in range(weight_ref.shape[0]):
        total_ref[...] += lax.dot_general(
            weight_ref[b],
            grad_ref[:, b * width : (b + 1) * width],
            (((1,), (1,)), ((), ())),
            preferred_element_type=jnp.float32,
        )

    @pl.when(step == pl.num_programs(0) - 1)
    def _():
        gate = gate_ref[...].astype(jnp.float32)
        up = up_ref[...].astype(jnp.float32)
        sigmoid = jax.nn.sigmoid(gate)
        hidden_grad = total_ref[...]
        up_grad_ref[...] = (hidden_grad * (gate * sigmoid)).astype(jnp.bfloat16)
        gate_grad_ref[...] = (
            hidden_grad * up * sigmoid * (1.0 + gate * (1.0 - sigmoid))
        ).astype(jnp.bfloat16)


def product(all_grad, weight, gate, up):
    blocks, rows, width = weight.shape
    tokens, features = all_grad.shape
    per_step = 2
    whole = pl.BlockSpec((rows, tokens), lambda k: (0, 0))
    return pl.pallas_call(
        product_kernel,
        grid=(blocks // per_step,),
        in_specs=[
            pl.BlockSpec((tokens, per_step * width), lambda k: (0, k)),
            pl.BlockSpec((per_step, rows, width), lambda k: (k, 0, 0)),
            whole,
            whole,
        ],
        out_specs=[whole, whole],
        out_shape=[jax.ShapeDtypeStruct((rows, tokens), jnp.bfloat16)] * 2,
        scratch_shapes=[pltpu.VMEM((rows, tokens), jnp.float32)],
        compiler_params=pltpu.CompilerParams(dimension_semantics=("arbitrary",)),
        cost_estimate=pl.CostEstimate(
            flops=2 * rows * tokens * features,
            bytes_accessed=2 * (tokens + rows) * features + 8 * rows * tokens,
            transcendentals=rows * tokens,
        ),
    )(all_grad, weight, gate, up)


def per_device(out_grad, gate_pre, up_pre, down_weight, momentum, band_index, band_count):
    worker_rows = gate_pre.shape[0]
    own_rows = gate_pre.shape[1]
    window = momentum.shape[2]
    workers = lax.axis_size(DP)
    block_count = band_index.shape[1]
    length = own_rows * window // block_count
    features = out_grad.shape[1]

    window_grad = gathered(out_grad[:, :window], FSDP).reshape(worker_rows, window)
    weight = lax.all_gather(down_weight, DP)
    all_grad = gathered_over_x(gathered_over_y(out_grad)).reshape(worker_rows, features)

    gate_float = gate_pre.astype(jnp.float32)
    hidden = (gate_float * jax.nn.sigmoid(gate_float) * up_pre.astype(jnp.float32)).astype(
        jnp.bfloat16
    )
    grad_scale = 1.0 / math.sqrt(worker_rows)
    worker_grad = (
        lax.dot_general(
            hidden, window_grad, (((0,), (0,)), ((), ())), preferred_element_type=jnp.float32
        )
        * grad_scale
    )
    slot_list = band_index[0]
    slot_ids = jnp.arange(slot_list.shape[1], dtype=jnp.int32)
    used = jnp.where(slot_ids[None, :] < band_count[0][:, None], slot_list, -1)
    frequency = jnp.arange(length, dtype=jnp.int32)
    mask = jnp.any(used[:, :, None] == frequency[None, None, :], axis=1)

    cosine_table = cosine_matrix(length)
    mixed = momentum_decay * momentum[0] + worker_grad
    spectrum = jnp.dot(mixed, cosine_table.T, precision=lax.Precision.HIGHEST)
    sent = jnp.where(mask, spectrum, 0.0)
    new_momentum = mixed - jnp.dot(sent, cosine_table, precision=lax.Precision.HIGHEST)

    share = -(-block_count // workers)
    share = -(-share // 8) * 8
    padded = jnp.pad(sent, ((0, share * workers - block_count), (0, 0)))
    parts = lax.all_to_all(padded.reshape(workers, share, length), DP, 0, 0)
    averaged = parts.sum(0) / workers
    own_update = jnp.dot(averaged, cosine_table, precision=lax.Precision.HIGHEST)
    update = gathered(own_update, DP).reshape(workers * share, length)[:block_count]

    gate_grad, up_grad = product(all_grad, weight, gate_pre.T, up_pre.T)
    return (gate_grad.T, up_grad.T, new_momentum[None], update)


def solution(mesh):
    torus = Mesh(mesh.devices.reshape(8, 2, 8, 4), ("z", "core", "y", "x"))
    both = ("z", "core", "y", "x")
    return jax.shard_map(
        per_device,
        mesh=torus,
        in_specs=(
            P(both, None),
            P(DP, FSDP),
            P(DP, FSDP),
            P(FSDP, DP),
            P(DP, FSDP, None),
            P(DP, FSDP, None),
            P(DP, FSDP),
        ),
        out_specs=(P(DP, FSDP), P(DP, FSDP), P(DP, FSDP, None), P(FSDP, None)),
        check_vma=False,
    )
```

```python
import math

import jax
import jax.numpy as jnp
from jax import lax
from jax.experimental import pallas as pl
from jax.experimental.pallas import tpu as pltpu
from jax.sharding import Mesh
from jax.sharding import PartitionSpec as P


DP = ("z", "core")
FSDP = ("y", "x")
momentum_decay = 0.9


def cosine_matrix(length):
    frequency = jnp.arange(length, dtype=jnp.int32).astype(jnp.float32)[:, None]
    position = jnp.arange(length, dtype=jnp.int32).astype(jnp.float32)[None, :]
    angles = math.pi * (position + 0.5) * frequency / length
    row_weight = jnp.where(frequency == 0.0, math.sqrt(1.0 / length), math.sqrt(2.0 / length))
    return jnp.cos(angles) * row_weight


def gathered(value, axis):
    count = lax.axis_size(axis)
    copies = jnp.broadcast_to(value[None], (count, *value.shape))
    return lax.all_to_all(copies, axis, 0, 0)


def product_kernel(order_ref, *refs):
    pieces, refs = refs[:4], refs[4:]
    weight_ref, gate_ref, up_ref, gate_grad_ref, up_grad_ref, total_ref, act_ref, slope_ref, rows_ref = refs
    step = pl.program_id(0)
    last = pl.num_programs(0) - 1

    @pl.when(step == 0)
    def _():
        gate = gate_ref[...].astype(jnp.float32)
        sigmoid = jax.nn.sigmoid(gate)
        act_ref[...] = gate * sigmoid
        slope_ref[...] = up_ref[...].astype(jnp.float32) * sigmoid * (1.0 + gate * (1.0 - sigmoid))

    for i, piece in enumerate(pieces):
        rows_ref[:, order_ref[i]] = piece[...]
    width = weight_ref.shape[2]
    rows = rows_ref[...].reshape(-1, rows_ref.shape[3])
    total = None
    for b in range(weight_ref.shape[0]):
        term = lax.dot_general(
            weight_ref[b],
            rows[:, b * width : (b + 1) * width],
            (((1,), (1,)), ((), ())),
            preferred_element_type=jnp.float32,
        )
        total = term if total is None else total + term

    @pl.when(step == 0)
    def _():
        total_ref[...] = total

    @pl.when((step > 0) & (step < last))
    def _():
        total_ref[...] += total

    @pl.when(step == last)
    def _():
        hidden_grad = total_ref[...] + total
        up_grad_ref[...] = (hidden_grad * act_ref[...]).astype(jnp.bfloat16)
        gate_grad_ref[...] = (hidden_grad * slope_ref[...]).astype(jnp.bfloat16)


def product(order, pieces, weight, gate, up):
    blocks, rows, width = weight.shape
    tokens = gate.shape[1]
    groups, depth, features = pieces[0].shape
    per_step = blocks // 2
    whole = pl.BlockSpec((rows, tokens), lambda k, order: (0, 0))
    piece = pl.BlockSpec((groups, depth, per_step * width), lambda k, order: (0, 0, k))
    return pl.pallas_call(
        product_kernel,
        grid_spec=pltpu.PrefetchScalarGridSpec(
            num_scalar_prefetch=1,
            grid=(blocks // per_step,),
            in_specs=[piece] * 4
            + [pl.BlockSpec((per_step, rows, width), lambda k, order: (k, 0, 0)), whole, whole],
            out_specs=[whole, whole],
            scratch_shapes=[pltpu.VMEM((rows, tokens), jnp.float32)] * 3
            + [pltpu.VMEM((groups, 4, depth, per_step * width), jnp.bfloat16)],
        ),
        out_shape=[jax.ShapeDtypeStruct((rows, tokens), jnp.bfloat16)] * 2,
        compiler_params=pltpu.CompilerParams(dimension_semantics=("arbitrary",)),
        cost_estimate=pl.CostEstimate(
            flops=2 * rows * tokens * features,
            bytes_accessed=2 * (tokens + rows) * features + 8 * rows * tokens,
            transcendentals=rows * tokens,
        ),
    )(order, *pieces, weight, gate, up)


def per_device_body(out_grad, gate_pre, up_pre, down_weight, momentum, band_index, band_count):
    worker_rows = gate_pre.shape[0]
    own_rows = gate_pre.shape[1]
    window = momentum.shape[2]
    workers = lax.axis_size(DP)
    block_count = band_index.shape[1]
    length = own_rows * window // block_count

    window_grad = gathered(out_grad[:, :window], FSDP).reshape(worker_rows, window)
    weight = lax.all_gather(down_weight, DP)
    own_piece = gathered(out_grad, "y")
    shifts = (0, 1, 3, 2)
    order = (lax.axis_index("x") + 4 - jnp.array(shifts, jnp.int32)) & 3
    pieces = [own_piece]
    for s in shifts[1:]:
        pieces.append(lax.ppermute(own_piece, "x", [(i, (i + s) % 4) for i in range(4)]))

    gate_float = gate_pre.astype(jnp.float32)
    hidden = (gate_float * jax.nn.sigmoid(gate_float) * up_pre.astype(jnp.float32)).astype(
        jnp.bfloat16
    )
    grad_scale = 1.0 / math.sqrt(worker_rows)
    worker_grad = (
        lax.dot_general(
            hidden, window_grad, (((0,), (0,)), ((), ())), preferred_element_type=jnp.float32
        )
        * grad_scale
    )
    slot_list = band_index[0]
    slot_ids = jnp.arange(slot_list.shape[1], dtype=jnp.int32)
    used = jnp.where(slot_ids[None, :] < band_count[0][:, None], slot_list, -1)
    frequency = jnp.arange(length, dtype=jnp.int32)
    mask = jnp.any(used[:, :, None] == frequency[None, None, :], axis=1)

    cosine_table = cosine_matrix(length)
    mixed = momentum_decay * momentum[0] + worker_grad
    spectrum = jnp.dot(mixed, cosine_table.T, precision=lax.Precision.HIGHEST)
    sent = jnp.where(mask, spectrum, 0.0)
    new_momentum = mixed - jnp.dot(sent, cosine_table, precision=lax.Precision.HIGHEST)

    share = -(-block_count // workers)
    share = -(-share // 8) * 8
    padded = jnp.pad(sent, ((0, share * workers - block_count), (0, 0)))
    parts = lax.all_to_all(padded.reshape(workers, share, length), DP, 0, 0)
    averaged = parts.sum(0) / workers
    own_update = jnp.dot(averaged, cosine_table, precision=lax.Precision.HIGHEST)
    update = gathered(own_update, DP).reshape(workers * share, length)[:block_count]

    gate_grad, up_grad = product(order, pieces, weight, gate_pre.T, up_pre.T)
    return (gate_grad.T, up_grad.T, new_momentum[None], update)


def solution(mesh):
    torus = Mesh(mesh.devices.reshape(8, 2, 8, 4), ("z", "core", "y", "x"))
    both = ("z", "core", "y", "x")
    return jax.shard_map(
        per_device_body,
        mesh=torus,
        in_specs=(
            P(both, None),
            P(DP, FSDP),
            P(DP, FSDP),
            P(FSDP, DP),
            P(DP, FSDP, None),
            P(DP, FSDP, None),
            P(DP, FSDP),
        ),
        out_specs=(P(DP, FSDP), P(DP, FSDP), P(DP, FSDP, None), P(FSDP, None)),
        check_vma=False,
    )
```

```python
import math

import jax
import jax.numpy as jnp
from jax import lax
from jax.experimental import pallas as pl
from jax.experimental.pallas import tpu as pltpu
from jax.sharding import Mesh
from jax.sharding import PartitionSpec as P


DP = ("z", "core")
FSDP = ("y", "x")
momentum_decay = 0.9


def cosine_matrix(length):
    frequency = jnp.arange(length, dtype=jnp.int32).astype(jnp.float32)[:, None]
    position = jnp.arange(length, dtype=jnp.int32).astype(jnp.float32)[None, :]
    angles = math.pi * (position + 0.5) * frequency / length
    row_weight = jnp.where(frequency == 0.0, math.sqrt(1.0 / length), math.sqrt(2.0 / length))
    return jnp.cos(angles) * row_weight


def gathered(value, axis):
    count = lax.axis_size(axis)
    copies = jnp.broadcast_to(value[None], (count, *value.shape))
    return lax.all_to_all(copies, axis, 0, 0)


def gathered_over_y(value):
    me = lax.axis_index("y")
    even = (me & 1) == 0
    blocks = jnp.zeros((4, 2, *value.shape), value.dtype)

    def put(blocks, pair, at):
        return lax.dynamic_update_slice(blocks, pair[None], (at, 0, 0, 0))

    got = lax.ppermute(value, "y", [(i, i ^ 1) for i in range(8)])
    pair = jnp.where(even, jnp.stack([value, got]), jnp.stack([got, value]))
    own = me >> 1
    blocks = put(blocks, pair, own)
    links = [(i, (i - 1) % 8 if i % 2 == 0 else (i + 1) % 8) for i in range(8)]
    got_pair = lax.ppermute(pair, "y", links)
    blocks = put(blocks, got_pair, (own + jnp.where(even, 3, 1)) & 3)
    links = [(i, (i + 3) % 8 if i % 2 == 0 else (i - 3) % 8) for i in range(8)]
    got_four = lax.ppermute(jnp.stack([pair, got_pair]), "y", links)
    far = ((me + jnp.where(even, 3, 5)) & 7) >> 1
    blocks = put(blocks, got_four[0], far)
    blocks = put(blocks, got_four[1], (far + jnp.where(even, 1, 3)) & 3)
    return blocks.reshape(8, *value.shape)


def mask_kernel(index_ref, count_ref, mask_ref):
    slots, blocks = index_ref.shape
    length = mask_ref.shape[1]
    slot = lax.broadcasted_iota(jnp.int32, (slots, blocks), 0)
    used = jnp.where(slot < count_ref[...], index_ref[...], -1)
    frequency = lax.broadcasted_iota(jnp.int32, (length, blocks), 0)
    found = used[0:1] == frequency
    for j in range(1, slots):
        found = found | (used[j : j + 1] == frequency)
    mask_ref[...] = jnp.zeros_like(mask_ref)
    mask_ref[:blocks] = jnp.where(found, 1.0, 0.0).astype(jnp.float32).T


def band_mask(index, count, rows, length):
    slots, blocks = index.shape
    return pl.pallas_call(
        mask_kernel,
        out_shape=jax.ShapeDtypeStruct((rows, length), jnp.float32),
        cost_estimate=pl.CostEstimate(
            flops=2 * slots * blocks * length, bytes_accessed=4 * rows * length, transcendentals=0
        ),
    )(index, count)


def product_kernel(order_ref, *refs):
    pieces, refs = refs[:4], refs[4:]
    weight_ref, gate_ref, up_ref, gate_grad_ref, up_grad_ref, total_ref, act_ref, slope_ref, rows_ref = refs
    step = pl.program_id(0)
    last = pl.num_programs(0) - 1

    @pl.when(step == 0)
    def _():
        gate = gate_ref[...].astype(jnp.float32)
        sigmoid = jax.nn.sigmoid(gate)
        act_ref[...] = gate * sigmoid
        slope_ref[...] = up_ref[...].astype(jnp.float32) * sigmoid * (1.0 + gate * (1.0 - sigmoid))

    for i, piece in enumerate(pieces):
        rows_ref[:, order_ref[i]] = piece[...]
    width = weight_ref.shape[2]
    rows = rows_ref[...].reshape(-1, rows_ref.shape[3])
    total = None
    for b in range(weight_ref.shape[0]):
        term = lax.dot_general(
            weight_ref[b],
            rows[:, b * width : (b + 1) * width],
            (((1,), (1,)), ((), ())),
            preferred_element_type=jnp.float32,
        )
        total = term if total is None else total + term

    @pl.when(step == 0)
    def _():
        total_ref[...] = total

    @pl.when((step > 0) & (step < last))
    def _():
        total_ref[...] += total

    @pl.when(step == last)
    def _():
        hidden_grad = total_ref[...] + total
        up_grad_ref[...] = (hidden_grad * act_ref[...]).astype(jnp.bfloat16)
        gate_grad_ref[...] = (hidden_grad * slope_ref[...]).astype(jnp.bfloat16)


def product(order, pieces, weight, gate, up):
    blocks, rows, width = weight.shape
    tokens = gate.shape[1]
    groups, depth, features = pieces[0].shape
    per_step = blocks // 2
    whole = pl.BlockSpec((rows, tokens), lambda k, order: (0, 0))
    piece = pl.BlockSpec((groups, depth, per_step * width), lambda k, order: (0, 0, k))
    return pl.pallas_call(
        product_kernel,
        grid_spec=pltpu.PrefetchScalarGridSpec(
            num_scalar_prefetch=1,
            grid=(blocks // per_step,),
            in_specs=[piece] * 4
            + [pl.BlockSpec((per_step, rows, width), lambda k, order: (k, 0, 0)), whole, whole],
            out_specs=[whole, whole],
            scratch_shapes=[pltpu.VMEM((rows, tokens), jnp.float32)] * 3
            + [pltpu.VMEM((groups, 4, depth, per_step * width), jnp.bfloat16)],
        ),
        out_shape=[jax.ShapeDtypeStruct((rows, tokens), jnp.bfloat16)] * 2,
        compiler_params=pltpu.CompilerParams(dimension_semantics=("arbitrary",)),
        cost_estimate=pl.CostEstimate(
            flops=2 * rows * tokens * features,
            bytes_accessed=2 * (tokens + rows) * features + 8 * rows * tokens,
            transcendentals=rows * tokens,
        ),
    )(order, *pieces, weight, gate, up)


def per_device_body(out_grad, gate_pre, up_pre, down_weight, momentum, band_index, band_count):
    worker_rows = gate_pre.shape[0]
    own_rows = gate_pre.shape[1]
    window = momentum.shape[2]
    workers = lax.axis_size(DP)
    block_count = band_index.shape[1]
    length = own_rows * window // block_count

    window_grad = gathered(out_grad[:, :window], FSDP).reshape(worker_rows, window)
    weight = lax.all_gather(down_weight, DP)
    own_piece = gathered_over_y(out_grad)
    shifts = (0, 1, 3, 2)
    order = (lax.axis_index("x") + 4 - jnp.array(shifts, jnp.int32)) & 3
    pieces = [own_piece]
    for s in shifts[1:]:
        pieces.append(lax.ppermute(own_piece, "x", [(i, (i + s) % 4) for i in range(4)]))

    gate_float = gate_pre.astype(jnp.float32)
    hidden = (gate_float * jax.nn.sigmoid(gate_float) * up_pre.astype(jnp.float32)).astype(
        jnp.bfloat16
    )
    grad_scale = 1.0 / math.sqrt(worker_rows)
    worker_grad = grad_scale * lax.dot_general(
        hidden, window_grad, (((0,), (0,)), ((), ())), preferred_element_type=jnp.float32
    )
    share = -(-block_count // workers)
    share = -(-share // 8) * 8
    rows = share * workers
    mask = band_mask(band_index[0].T, band_count, rows, length)

    cosine_table = cosine_matrix(length)
    mixed = momentum_decay * momentum[0] + worker_grad
    spread = jnp.pad(mixed, ((0, rows - block_count), (0, 0)))
    spectrum = jnp.dot(spread, cosine_table.T, precision=lax.Precision.HIGHEST)
    sent = jnp.where(mask > 0.0, spectrum, 0.0)
    new_momentum = mixed - jnp.dot(
        sent[:block_count], cosine_table, precision=lax.Precision.HIGHEST
    )

    parts = lax.all_to_all(sent.reshape(workers, share, length), DP, 0, 0)
    averaged = parts.sum(0) / workers
    own_update = jnp.dot(averaged, cosine_table, precision=lax.Precision.HIGHEST)
    update = gathered(own_update, DP).reshape(rows, length)[:block_count]

    gate_grad, up_grad = product(order, pieces, weight, gate_pre.T, up_pre.T)
    return (gate_grad.T, up_grad.T, new_momentum[None], update)


def solution(mesh):
    torus = Mesh(mesh.devices.reshape(8, 2, 8, 4), ("z", "core", "y", "x"))
    both = ("z", "core", "y", "x")
    return jax.shard_map(
        per_device_body,
        mesh=torus,
        in_specs=(
            P(both, None),
            P(DP, FSDP),
            P(DP, FSDP),
            P(FSDP, DP),
            P(DP, FSDP, None),
            P(DP, FSDP, None),
            P(DP, FSDP),
        ),
        out_specs=(P(DP, FSDP), P(DP, FSDP), P(DP, FSDP, None), P(FSDP, None)),
        check_vma=False,
    )
```

```python
import math

import jax
import jax.numpy as jnp
from jax import lax
from jax.experimental import pallas as pl
from jax.experimental.pallas import tpu as pltpu
from jax.sharding import Mesh
from jax.sharding import PartitionSpec as P


DP = ("z", "core")
FSDP = ("y", "x")
momentum_decay = 0.9


def cosine_matrix(length):
    frequency = jnp.arange(length, dtype=jnp.int32).astype(jnp.float32)[:, None]
    position = jnp.arange(length, dtype=jnp.int32).astype(jnp.float32)[None, :]
    angles = math.pi * (position + 0.5) * frequency / length
    row_weight = jnp.where(frequency == 0.0, math.sqrt(1.0 / length), math.sqrt(2.0 / length))
    return jnp.cos(angles) * row_weight


def gathered(value, axis):
    count = lax.axis_size(axis)
    copies = jnp.broadcast_to(value[None], (count, *value.shape))
    return lax.all_to_all(copies, axis, 0, 0)


def gathered_over_y(value):
    me = lax.axis_index("y")
    even = (me & 1) == 0
    blocks = jnp.zeros((4, 2, *value.shape), value.dtype)

    def put(blocks, pair, at):
        return lax.dynamic_update_slice(blocks, pair[None], (at, 0, 0, 0))

    got = lax.ppermute(value, "y", [(i, i ^ 1) for i in range(8)])
    pair = jnp.where(even, jnp.stack([value, got]), jnp.stack([got, value]))
    own = me >> 1
    blocks = put(blocks, pair, own)
    links = [(i, (i - 1) % 8 if i % 2 == 0 else (i + 1) % 8) for i in range(8)]
    got_pair = lax.ppermute(pair, "y", links)
    blocks = put(blocks, got_pair, (own + jnp.where(even, 3, 1)) & 3)
    links = [(i, (i + 3) % 8 if i % 2 == 0 else (i - 3) % 8) for i in range(8)]
    got_four = lax.ppermute(jnp.stack([pair, got_pair]), "y", links)
    far = ((me + jnp.where(even, 3, 5)) & 7) >> 1
    blocks = put(blocks, got_four[0], far)
    blocks = put(blocks, got_four[1], (far + jnp.where(even, 1, 3)) & 3)
    return blocks.reshape(8, *value.shape)


def mask_kernel(index_ref, count_ref, mask_ref):
    slots, blocks = index_ref.shape
    length = mask_ref.shape[1]
    index = index_ref[...]
    slot = lax.broadcasted_iota(jnp.int32, (slots, blocks), 0)
    bit = jnp.where(slot < count_ref[...], lax.shift_left(jnp.ones_like(index), index & 31), 0)
    word = lax.shift_right_logical(index, 5)
    place = lax.broadcasted_iota(jnp.int32, (32, blocks), 0)
    parts = []
    for w in range(length // 32):
        value = jnp.sum(jnp.where(word == w, bit, 0), axis=0, keepdims=True)
        ones = lax.shift_right_logical(jnp.broadcast_to(value, place.shape), place) & 1
        parts.append(ones.astype(jnp.float32))
    mask_ref[...] = jnp.zeros_like(mask_ref)
    mask_ref[:blocks] = jnp.concatenate(parts, axis=0).T


def band_mask(index, count, rows, length):
    slots, blocks = index.shape
    return pl.pallas_call(
        mask_kernel,
        out_shape=jax.ShapeDtypeStruct((rows, length), jnp.float32),
        cost_estimate=pl.CostEstimate(
            flops=2 * slots * blocks * length, bytes_accessed=4 * rows * length, transcendentals=0
        ),
    )(index, count)


def product_kernel(order_ref, *refs):
    pieces, refs = refs[:4], refs[4:]
    weight_ref, gate_ref, up_ref, gate_grad_ref, up_grad_ref, total_ref, act_ref, slope_ref, rows_ref = refs
    step = pl.program_id(0)
    last = pl.num_programs(0) - 1

    @pl.when(step == 0)
    def _():
        gate = gate_ref[...].astype(jnp.float32)
        sigmoid = jax.nn.sigmoid(gate)
        act_ref[...] = gate * sigmoid
        slope_ref[...] = up_ref[...].astype(jnp.float32) * sigmoid * (1.0 + gate * (1.0 - sigmoid))

    for i, piece in enumerate(pieces):
        rows_ref[:, order_ref[i]] = piece[...]
    width = weight_ref.shape[2]
    rows = rows_ref[...].reshape(-1, rows_ref.shape[3])
    total = None
    for b in range(weight_ref.shape[0]):
        term = lax.dot_general(
            weight_ref[b],
            rows[:, b * width : (b + 1) * width],
            (((1,), (1,)), ((), ())),
            preferred_element_type=jnp.float32,
        )
        total = term if total is None else total + term

    @pl.when(step == 0)
    def _():
        total_ref[...] = total

    @pl.when((step > 0) & (step < last))
    def _():
        total_ref[...] += total

    @pl.when(step == last)
    def _():
        hidden_grad = total_ref[...] + total
        up_grad_ref[...] = (hidden_grad * act_ref[...]).astype(jnp.bfloat16)
        gate_grad_ref[...] = (hidden_grad * slope_ref[...]).astype(jnp.bfloat16)


def product(order, pieces, weight, gate, up):
    blocks, rows, width = weight.shape
    tokens = gate.shape[1]
    groups, depth, features = pieces[0].shape
    per_step = blocks // 2
    whole = pl.BlockSpec((rows, tokens), lambda k, order: (0, 0))
    piece = pl.BlockSpec((groups, depth, per_step * width), lambda k, order: (0, 0, k))
    return pl.pallas_call(
        product_kernel,
        grid_spec=pltpu.PrefetchScalarGridSpec(
            num_scalar_prefetch=1,
            grid=(blocks // per_step,),
            in_specs=[piece] * 4
            + [pl.BlockSpec((per_step, rows, width), lambda k, order: (k, 0, 0)), whole, whole],
            out_specs=[whole, whole],
            scratch_shapes=[pltpu.VMEM((rows, tokens), jnp.float32)] * 3
            + [pltpu.VMEM((groups, 4, depth, per_step * width), jnp.bfloat16)],
        ),
        out_shape=[jax.ShapeDtypeStruct((rows, tokens), jnp.bfloat16)] * 2,
        compiler_params=pltpu.CompilerParams(dimension_semantics=("arbitrary",)),
        cost_estimate=pl.CostEstimate(
            flops=2 * rows * tokens * features,
            bytes_accessed=2 * (tokens + rows) * features + 8 * rows * tokens,
            transcendentals=rows * tokens,
        ),
    )(order, *pieces, weight, gate, up)


def per_device_body(out_grad, gate_pre, up_pre, down_weight, momentum, band_index, band_count):
    worker_rows = gate_pre.shape[0]
    own_rows = gate_pre.shape[1]
    window = momentum.shape[2]
    workers = lax.axis_size(DP)
    block_count = band_index.shape[1]
    length = own_rows * window // block_count

    window_grad = gathered(out_grad[:, :window], FSDP).reshape(worker_rows, window)
    weight = lax.all_gather(down_weight, DP)
    own_piece = gathered_over_y(out_grad)
    shifts = (0, 1, 3, 2)
    order = (lax.axis_index("x") + 4 - jnp.array(shifts, jnp.int32)) & 3
    pieces = [own_piece]
    for s in shifts[1:]:
        pieces.append(lax.ppermute(own_piece, "x", [(i, (i + s) % 4) for i in range(4)]))

    gate_float = gate_pre.astype(jnp.float32)
    hidden = (gate_float * jax.nn.sigmoid(gate_float) * up_pre.astype(jnp.float32)).astype(
        jnp.bfloat16
    )
    grad_scale = 1.0 / math.sqrt(worker_rows)
    worker_grad = grad_scale * lax.dot_general(
        hidden, window_grad, (((0,), (0,)), ((), ())), preferred_element_type=jnp.float32
    )
    share = -(-block_count // workers)
    share = -(-share // 8) * 8
    rows = share * workers
    mask = band_mask(band_index[0].T, band_count, rows, length)

    cosine_table = cosine_matrix(length)
    mixed = momentum_decay * momentum[0] + worker_grad
    spread = jnp.pad(mixed, ((0, rows - block_count), (0, 0)))
    spectrum = jnp.dot(spread, cosine_table.T, precision=lax.Precision.HIGHEST)
    sent = jnp.where(mask > 0.0, spectrum, 0.0)
    new_momentum = mixed - jnp.dot(
        sent[:block_count], cosine_table, precision=lax.Precision.HIGHEST
    )

    parts = lax.all_to_all(sent.reshape(workers, share, length), DP, 0, 0)
    averaged = parts.sum(0) / workers
    own_update = jnp.dot(averaged, cosine_table, precision=lax.Precision.HIGHEST)
    update = gathered(own_update, DP).reshape(rows, length)[:block_count]

    gate_grad, up_grad = product(order, pieces, weight, gate_pre.T, up_pre.T)
    return (gate_grad.T, up_grad.T, new_momentum[None], update)


def solution(mesh):
    torus = Mesh(mesh.devices.reshape(8, 2, 8, 4), ("z", "core", "y", "x"))
    both = ("z", "core", "y", "x")
    return jax.shard_map(
        per_device_body,
        mesh=torus,
        in_specs=(
            P(both, None),
            P(DP, FSDP),
            P(DP, FSDP),
            P(FSDP, DP),
            P(DP, FSDP, None),
            P(DP, FSDP, None),
            P(DP, FSDP),
        ),
        out_specs=(P(DP, FSDP), P(DP, FSDP), P(DP, FSDP, None), P(FSDP, None)),
        check_vma=False,
    )
```

```python
import math

import jax
import jax.numpy as jnp
import numpy as np
from jax import lax
from jax.experimental import pallas as pl
from jax.experimental.pallas import tpu as pltpu
from jax.sharding import Mesh
from jax.sharding import PartitionSpec as P


DP = ("z", "core")
FSDP = ("y", "x")
momentum_decay = 0.9
SHIFTS = (0, 1, 3, 2)


def cosine_matrix(length):
    frequency = np.arange(length, dtype=np.float64)[:, None]
    position = np.arange(length, dtype=np.float64)[None, :]
    row_weight = np.where(frequency == 0.0, math.sqrt(1.0 / length), math.sqrt(2.0 / length))
    return (np.cos(math.pi * (position + 0.5) * frequency / length) * row_weight).astype(np.float32)


def gathered(value, axis):
    count = lax.axis_size(axis)
    copies = jnp.broadcast_to(value[None], (count, *value.shape))
    return lax.all_to_all(copies, axis, 0, 0)


def gathered_over_y(value):
    near = lax.ppermute(value, "y", [(i, i ^ 1) for i in range(8)])
    pair = jnp.stack([value, near])
    links = [(i, (i - 1) % 8 if i % 2 == 0 else (i + 1) % 8) for i in range(8)]
    second = lax.ppermute(pair, "y", links)
    four = jnp.concatenate([pair, second])
    links = [(i, (i + 3) % 8 if i % 2 == 0 else (i - 3) % 8) for i in range(8)]
    third = lax.ppermute(four, "y", links)
    return jnp.concatenate([four, third])


def arrival_order():
    def second(y):
        return (y - 1) % 8 if y % 2 == 0 else (y + 1) % 8

    def third(y):
        return (y + 3) % 8 if y % 2 == 0 else (y - 3) % 8

    table = []
    for y in range(8):
        pairs = [y, second(y), third(y), second(third(y))]
        blocks = [b for p in pairs for b in (p, p ^ 1)]
        table += [[(x - s) % 4 for s in SHIFTS] + blocks for x in range(4)]
    row = lax.axis_index("y") * 4 + lax.axis_index("x")
    table = jnp.asarray(np.array(table, np.int32))
    return lax.dynamic_slice(table, (row, 0), (1, table.shape[1]))[0]


def mask_kernel(index_ref, count_ref, mask_ref):
    slots, blocks = index_ref.shape
    length = mask_ref.shape[1]
    index = index_ref[...]
    slot = lax.broadcasted_iota(jnp.int32, (slots, blocks), 0)
    bit = jnp.where(slot < count_ref[...], lax.shift_left(jnp.ones_like(index), index & 31), 0)
    word = lax.shift_right_logical(index, 5)
    place = lax.broadcasted_iota(jnp.int32, (32, blocks), 0)
    parts = []
    for w in range(length // 32):
        value = jnp.sum(jnp.where(word == w, bit, 0), axis=0, keepdims=True)
        ones = lax.shift_right_logical(jnp.broadcast_to(value, place.shape), place) & 1
        parts.append(ones.astype(jnp.float32))
    mask_ref[...] = jnp.zeros_like(mask_ref)
    mask_ref[:blocks] = jnp.concatenate(parts, axis=0).T


def band_mask(index, count, rows, length):
    slots, blocks = index.shape
    return pl.pallas_call(
        mask_kernel,
        out_shape=jax.ShapeDtypeStruct((rows, length), jnp.float32),
        cost_estimate=pl.CostEstimate(
            flops=2 * slots * blocks * length, bytes_accessed=4 * rows * length, transcendentals=0
        ),
    )(index, count)


def product_kernel(order_ref, *refs):
    pieces, refs = refs[:4], refs[4:]
    weight_ref, gate_ref, up_ref, gate_grad_ref, up_grad_ref, total_ref, act_ref, slope_ref, rows_ref = refs
    step = pl.program_id(0)
    last = pl.num_programs(0) - 1

    @pl.when(step == 0)
    def _():
        gate = gate_ref[...].astype(jnp.float32)
        sigmoid = jax.nn.sigmoid(gate)
        act_ref[...] = gate * sigmoid
        slope_ref[...] = up_ref[...].astype(jnp.float32) * sigmoid * (1.0 + gate * (1.0 - sigmoid))

    for i, piece in enumerate(pieces):
        for j in range(piece.shape[0]):
            rows_ref[order_ref[4 + j], order_ref[i]] = piece[j]
    width = weight_ref.shape[2]
    rows = rows_ref[...].reshape(-1, rows_ref.shape[3])
    total = None
    for b in range(weight_ref.shape[0]):
        term = lax.dot_general(
            weight_ref[b],
            rows[:, b * width : (b + 1) * width],
            (((1,), (1,)), ((), ())),
            preferred_element_type=jnp.float32,
        )
        total = term if total is None else total + term

    @pl.when(step == 0)
    def _():
        total_ref[...] = total

    @pl.when((step > 0) & (step < last))
    def _():
        total_ref[...] += total

    @pl.when(step == last)
    def _():
        hidden_grad = total_ref[...] + total
        up_grad_ref[...] = (hidden_grad * act_ref[...]).astype(jnp.bfloat16)
        gate_grad_ref[...] = (hidden_grad * slope_ref[...]).astype(jnp.bfloat16)


def product(order, pieces, weight, gate, up):
    blocks, rows, width = weight.shape
    tokens = gate.shape[1]
    groups, depth, features = pieces[0].shape
    per_step = blocks // 2
    whole = pl.BlockSpec((rows, tokens), lambda k, order: (0, 0))
    piece = pl.BlockSpec((groups, depth, per_step * width), lambda k, order: (0, 0, k))
    return pl.pallas_call(
        product_kernel,
        grid_spec=pltpu.PrefetchScalarGridSpec(
            num_scalar_prefetch=1,
            grid=(blocks // per_step,),
            in_specs=[piece] * 4
            + [pl.BlockSpec((per_step, rows, width), lambda k, order: (k, 0, 0)), whole, whole],
            out_specs=[whole, whole],
            scratch_shapes=[pltpu.VMEM((rows, tokens), jnp.float32)] * 3
            + [pltpu.VMEM((groups, 4, depth, per_step * width), jnp.bfloat16)],
        ),
        out_shape=[jax.ShapeDtypeStruct((rows, tokens), jnp.bfloat16)] * 2,
        compiler_params=pltpu.CompilerParams(dimension_semantics=("arbitrary",)),
        cost_estimate=pl.CostEstimate(
            flops=2 * rows * tokens * features,
            bytes_accessed=2 * (tokens + rows) * features + 8 * rows * tokens,
            transcendentals=rows * tokens,
        ),
    )(order, *pieces, weight, gate, up)


def per_device_body(out_grad, gate_pre, up_pre, down_weight, momentum, band_index, band_count):
    worker_rows = gate_pre.shape[0]
    own_rows = gate_pre.shape[1]
    window = momentum.shape[2]
    workers = lax.axis_size(DP)
    block_count = band_index.shape[1]
    length = own_rows * window // block_count

    window_grad = gathered(out_grad[:, :window], FSDP).reshape(worker_rows, window)
    weight = lax.all_gather(down_weight, DP)
    own_piece = gathered_over_y(out_grad)
    order = arrival_order()
    pieces = [own_piece]
    for s in SHIFTS[1:]:
        pieces.append(lax.ppermute(own_piece, "x", [(i, (i + s) % 4) for i in range(4)]))

    gate_float = gate_pre.astype(jnp.float32)
    hidden = (gate_float * jax.nn.sigmoid(gate_float) * up_pre.astype(jnp.float32)).astype(
        jnp.bfloat16
    )
    grad_scale = 1.0 / math.sqrt(worker_rows)
    worker_grad = grad_scale * lax.dot_general(
        hidden, window_grad, (((0,), (0,)), ((), ())), preferred_element_type=jnp.float32
    )
    share = -(-block_count // workers)
    share = -(-share // 8) * 8
    rows = share * workers
    mask = band_mask(band_index[0].T, band_count, rows, length)

    cosine_table = jnp.asarray(cosine_matrix(length))
    mixed = momentum_decay * momentum[0] + worker_grad
    spread = jnp.pad(mixed, ((0, rows - block_count), (0, 0)))
    spectrum = jnp.dot(spread, cosine_table.T, precision=lax.Precision.HIGH)
    sent = jnp.where(mask > 0.0, spectrum, 0.0)
    new_momentum = mixed - jnp.dot(sent[:block_count], cosine_table, precision=lax.Precision.HIGH)

    parts = lax.all_to_all(sent.reshape(workers, share, length), DP, 0, 0)
    averaged = parts.sum(0) / workers
    own_update = jnp.dot(averaged, cosine_table, precision=lax.Precision.HIGH)
    update = gathered(own_update, DP).reshape(rows, length)[:block_count]

    gate_grad, up_grad = product(order, pieces, weight, gate_pre.T, up_pre.T)
    return (gate_grad.T, up_grad.T, new_momentum[None], update)


def solution(mesh):
    torus = Mesh(mesh.devices.reshape(8, 2, 8, 4), ("z", "core", "y", "x"))
    both = ("z", "core", "y", "x")
    return jax.shard_map(
        per_device_body,
        mesh=torus,
        in_specs=(
            P(both, None),
            P(DP, FSDP),
            P(DP, FSDP),
            P(FSDP, DP),
            P(DP, FSDP, None),
            P(DP, FSDP, None),
            P(DP, FSDP),
        ),
        out_specs=(P(DP, FSDP), P(DP, FSDP), P(DP, FSDP, None), P(FSDP, None)),
        check_vma=False,
    )
```

```python
import math

import jax
import jax.numpy as jnp
import numpy as np
from jax import lax
from jax.experimental import pallas as pl
from jax.experimental.pallas import tpu as pltpu
from jax.sharding import Mesh
from jax.sharding import PartitionSpec as P


DP = ("z", "core")
FSDP = ("y", "x")
momentum_decay = 0.9
SHIFTS = (0, 1, 3, 2)


def cosine_matrix(length):
    frequency = np.arange(length, dtype=np.float64)[:, None]
    position = np.arange(length, dtype=np.float64)[None, :]
    row_weight = np.where(frequency == 0.0, math.sqrt(1.0 / length), math.sqrt(2.0 / length))
    return (np.cos(math.pi * (position + 0.5) * frequency / length) * row_weight).astype(np.float32)


def gathered(value, axis):
    count = lax.axis_size(axis)
    copies = jnp.broadcast_to(value[None], (count, *value.shape))
    return lax.all_to_all(copies, axis, 0, 0)


def gathered_over_y(value):
    near = lax.ppermute(value, "y", [(i, i ^ 1) for i in range(8)])
    pair = jnp.stack([value, near])
    links = [(i, (i - 1) % 8 if i % 2 == 0 else (i + 1) % 8) for i in range(8)]
    second = lax.ppermute(pair, "y", links)
    four = jnp.concatenate([pair, second])
    links = [(i, (i + 3) % 8 if i % 2 == 0 else (i - 3) % 8) for i in range(8)]
    third = lax.ppermute(four, "y", links)
    return jnp.concatenate([four, third])


def arrival_order():
    def second(y):
        return (y - 1) % 8 if y % 2 == 0 else (y + 1) % 8

    def third(y):
        return (y + 3) % 8 if y % 2 == 0 else (y - 3) % 8

    table = []
    for y in range(8):
        pairs = [y, second(y), third(y), second(third(y))]
        blocks = [b for p in pairs for b in (p, p ^ 1)]
        table += [[(x - s) % 4 for s in SHIFTS] + blocks for x in range(4)]
    row = lax.axis_index("y") * 4 + lax.axis_index("x")
    table = jnp.asarray(np.array(table, np.int32))
    return lax.dynamic_slice(table, (row, 0), (1, table.shape[1]))[0]


def mask_kernel(index_ref, count_ref, mask_ref):
    slots, blocks = index_ref.shape
    length = mask_ref.shape[1]
    index = index_ref[...]
    slot = lax.broadcasted_iota(jnp.int32, (slots, blocks), 0)
    bit = jnp.where(slot < count_ref[...], lax.shift_left(jnp.ones_like(index), index & 31), 0)
    word = lax.shift_right_logical(index, 5)
    place = lax.broadcasted_iota(jnp.int32, (32, blocks), 0)
    parts = []
    for w in range(length // 32):
        value = jnp.sum(jnp.where(word == w, bit, 0), axis=0, keepdims=True)
        ones = lax.shift_right_logical(jnp.broadcast_to(value, place.shape), place) & 1
        parts.append(ones.astype(jnp.float32))
    mask_ref[...] = jnp.zeros_like(mask_ref)
    mask_ref[:blocks] = jnp.concatenate(parts, axis=0).T


def band_mask(index, count, rows, length):
    slots, blocks = index.shape
    return pl.pallas_call(
        mask_kernel,
        out_shape=jax.ShapeDtypeStruct((rows, length), jnp.float32),
        cost_estimate=pl.CostEstimate(
            flops=2 * slots * blocks * length, bytes_accessed=4 * rows * length, transcendentals=0
        ),
    )(index, count)


def interleave_kernel(core_ref, own_ref, other_ref, out_ref):
    core = core_ref[0]
    count, share, _ = own_ref.shape
    for z in range(count):
        first = 2 * z * share
        if first + 2 * share <= out_ref.shape[0]:
            out_ref[pl.ds(pl.multiple_of(first + core * share, share), share)] = own_ref[z]
            out_ref[pl.ds(pl.multiple_of(first + (1 - core) * share, share), share)] = other_ref[z]
        else:
            left = out_ref.shape[0] - first
            even = jnp.where(core == 0, own_ref[z], other_ref[z])
            odd = jnp.where(core == 0, other_ref[z], own_ref[z])
            out_ref[first:] = jnp.concatenate([even, odd], axis=0)[:left]


def interleaved(core, own, other, rows):
    whole = pl.BlockSpec(own.shape, lambda i, core: (0, 0, 0))
    return pl.pallas_call(
        interleave_kernel,
        grid_spec=pltpu.PrefetchScalarGridSpec(
            num_scalar_prefetch=1,
            grid=(1,),
            in_specs=[whole, whole],
            out_specs=pl.BlockSpec((rows, own.shape[2]), lambda i, core: (0, 0)),
        ),
        out_shape=jax.ShapeDtypeStruct((rows, own.shape[2]), own.dtype),
    )(core.reshape(1), own, other)


def product_kernel(order_ref, *refs):
    pieces, refs = refs[:4], refs[4:]
    weight_ref, gate_ref, up_ref, gate_grad_ref, up_grad_ref, total_ref, act_ref, slope_ref, rows_ref = refs
    step = pl.program_id(0)
    last = pl.num_programs(0) - 1

    @pl.when(step == 0)
    def _():
        gate = gate_ref[...].astype(jnp.float32)
        sigmoid = jax.nn.sigmoid(gate)
        act_ref[...] = gate * sigmoid
        slope_ref[...] = up_ref[...].astype(jnp.float32) * sigmoid * (1.0 + gate * (1.0 - sigmoid))

    for i, piece in enumerate(pieces):
        for j in range(piece.shape[0]):
            rows_ref[order_ref[4 + j], order_ref[i]] = piece[j]
    width = weight_ref.shape[2]
    rows = rows_ref[...].reshape(-1, rows_ref.shape[3])
    total = None
    for b in range(weight_ref.shape[0]):
        term = lax.dot_general(
            weight_ref[b],
            rows[:, b * width : (b + 1) * width],
            (((1,), (1,)), ((), ())),
            preferred_element_type=jnp.float32,
        )
        total = term if total is None else total + term

    @pl.when(step == 0)
    def _():
        total_ref[...] = total

    @pl.when((step > 0) & (step < last))
    def _():
        total_ref[...] += total

    @pl.when(step == last)
    def _():
        hidden_grad = total_ref[...] + total
        up_grad_ref[...] = (hidden_grad * act_ref[...]).astype(jnp.bfloat16)
        gate_grad_ref[...] = (hidden_grad * slope_ref[...]).astype(jnp.bfloat16)


def product(order, pieces, weight, gate, up):
    blocks, rows, width = weight.shape
    tokens = gate.shape[1]
    groups, depth, features = pieces[0].shape
    per_step = blocks // 2
    whole = pl.BlockSpec((rows, tokens), lambda k, order: (0, 0))
    piece = pl.BlockSpec((groups, depth, per_step * width), lambda k, order: (0, 0, k))
    return pl.pallas_call(
        product_kernel,
        grid_spec=pltpu.PrefetchScalarGridSpec(
            num_scalar_prefetch=1,
            grid=(blocks // per_step,),
            in_specs=[piece] * 4
            + [pl.BlockSpec((per_step, rows, width), lambda k, order: (k, 0, 0)), whole, whole],
            out_specs=[whole, whole],
            scratch_shapes=[pltpu.VMEM((rows, tokens), jnp.float32)] * 3
            + [pltpu.VMEM((groups, 4, depth, per_step * width), jnp.bfloat16)],
        ),
        out_shape=[jax.ShapeDtypeStruct((rows, tokens), jnp.bfloat16)] * 2,
        compiler_params=pltpu.CompilerParams(dimension_semantics=("arbitrary",)),
        cost_estimate=pl.CostEstimate(
            flops=2 * rows * tokens * features,
            bytes_accessed=2 * (tokens + rows) * features + 8 * rows * tokens,
            transcendentals=rows * tokens,
        ),
    )(order, *pieces, weight, gate, up)


def per_device_body(out_grad, gate_pre, up_pre, down_weight, momentum, band_index, band_count):
    worker_rows = gate_pre.shape[0]
    own_rows = gate_pre.shape[1]
    window = momentum.shape[2]
    workers = lax.axis_size(DP)
    block_count = band_index.shape[1]
    length = own_rows * window // block_count

    window_grad = gathered(out_grad[:, :window], FSDP).reshape(worker_rows, window)
    weight = lax.all_gather(down_weight, DP)
    own_piece = gathered_over_y(out_grad)
    order = arrival_order()
    pieces = [own_piece]
    for s in SHIFTS[1:]:
        pieces.append(lax.ppermute(own_piece, "x", [(i, (i + s) % 4) for i in range(4)]))

    gate_float = gate_pre.astype(jnp.float32)
    hidden = (gate_float * jax.nn.sigmoid(gate_float) * up_pre.astype(jnp.float32)).astype(
        jnp.bfloat16
    )
    grad_scale = 1.0 / math.sqrt(worker_rows)
    worker_grad = grad_scale * lax.dot_general(
        hidden, window_grad, (((0,), (0,)), ((), ())), preferred_element_type=jnp.float32
    )
    share = -(-block_count // workers)
    share = -(-share // 8) * 8
    rows = share * workers
    mask = band_mask(band_index[0].T, band_count, rows, length)

    cosine_table = jnp.asarray(cosine_matrix(length))
    mixed = momentum_decay * momentum[0] + worker_grad
    spread = jnp.pad(mixed, ((0, rows - block_count), (0, 0)))
    spectrum = jnp.dot(spread, cosine_table.T, precision=lax.Precision.HIGH)
    sent = jnp.where(mask > 0.0, spectrum, 0.0)
    new_momentum = mixed - jnp.dot(sent[:block_count], cosine_table, precision=lax.Precision.HIGH)

    parts = lax.all_to_all(sent.reshape(workers, share, length), DP, 0, 0)
    averaged = parts.sum(0) / workers
    own_update = jnp.dot(averaged, cosine_table, precision=lax.Precision.HIGH)
    along_z = gathered(own_update, "z")
    swapped = lax.ppermute(along_z, "core", [(0, 1), (1, 0)])
    update = interleaved(lax.axis_index("core"), along_z, swapped, block_count)

    gate_grad, up_grad = product(order, pieces, weight, gate_pre.T, up_pre.T)
    return (gate_grad.T, up_grad.T, new_momentum[None], update)


def solution(mesh):
    torus = Mesh(mesh.devices.reshape(8, 2, 8, 4), ("z", "core", "y", "x"))
    both = ("z", "core", "y", "x")
    return jax.shard_map(
        per_device_body,
        mesh=torus,
        in_specs=(
            P(both, None),
            P(DP, FSDP),
            P(DP, FSDP),
            P(FSDP, DP),
            P(DP, FSDP, None),
            P(DP, FSDP, None),
            P(DP, FSDP),
        ),
        out_specs=(P(DP, FSDP), P(DP, FSDP), P(DP, FSDP, None), P(FSDP, None)),
        check_vma=False,
    )
```

```python
import math

import jax
import jax.numpy as jnp
import numpy as np
from jax import lax
from jax.experimental import pallas as pl
from jax.experimental.pallas import tpu as pltpu
from jax.sharding import Mesh
from jax.sharding import PartitionSpec as P


DP = ("z", "core")
FSDP = ("y", "x")
momentum_decay = 0.9
SHIFTS = (0, 1, 3, 2)


def cosine_matrix(length):
    frequency = np.arange(length, dtype=np.float64)[:, None]
    position = np.arange(length, dtype=np.float64)[None, :]
    row_weight = np.where(frequency == 0.0, math.sqrt(1.0 / length), math.sqrt(2.0 / length))
    return (np.cos(math.pi * (position + 0.5) * frequency / length) * row_weight).astype(np.float32)


def gathered(value, axis):
    count = lax.axis_size(axis)
    copies = jnp.broadcast_to(value[None], (count, *value.shape))
    return lax.all_to_all(copies, axis, 0, 0)


def gathered_over_y(value):
    near = lax.ppermute(value, "y", [(i, i ^ 1) for i in range(8)])
    pair = jnp.stack([value, near])
    links = [(i, (i - 1) % 8 if i % 2 == 0 else (i + 1) % 8) for i in range(8)]
    second = lax.ppermute(pair, "y", links)
    four = jnp.concatenate([pair, second])
    links = [(i, (i + 3) % 8 if i % 2 == 0 else (i - 3) % 8) for i in range(8)]
    third = lax.ppermute(four, "y", links)
    return jnp.concatenate([four, third])


def arrival_order():
    def second(y):
        return (y - 1) % 8 if y % 2 == 0 else (y + 1) % 8

    def third(y):
        return (y + 3) % 8 if y % 2 == 0 else (y - 3) % 8

    table = []
    for y in range(8):
        pairs = [y, second(y), third(y), second(third(y))]
        blocks = [b for p in pairs for b in (p, p ^ 1)]
        table += [[(x - s) % 4 for s in SHIFTS] + blocks for x in range(4)]
    row = lax.axis_index("y") * 4 + lax.axis_index("x")
    table = jnp.asarray(np.array(table, np.int32))
    return lax.dynamic_slice(table, (row, 0), (1, table.shape[1]))[0]


def mask_kernel(index_ref, count_ref, mask_ref):
    slots, blocks = index_ref.shape
    length = mask_ref.shape[1]
    index = index_ref[...]
    slot = lax.broadcasted_iota(jnp.int32, (slots, blocks), 0)
    bit = jnp.where(slot < count_ref[...], lax.shift_left(jnp.ones_like(index), index & 31), 0)
    word = lax.shift_right_logical(index, 5)
    place = lax.broadcasted_iota(jnp.int32, (32, blocks), 0)
    parts = []
    for w in range(length // 32):
        value = jnp.sum(jnp.where(word == w, bit, 0), axis=0, keepdims=True)
        ones = lax.shift_right_logical(jnp.broadcast_to(value, place.shape), place) & 1
        parts.append(ones.astype(jnp.float32))
    mask_ref[...] = jnp.zeros_like(mask_ref)
    mask_ref[:blocks] = jnp.concatenate(parts, axis=0).T


def band_mask(index, count, rows, length):
    slots, blocks = index.shape
    return pl.pallas_call(
        mask_kernel,
        out_shape=jax.ShapeDtypeStruct((rows, length), jnp.float32),
        cost_estimate=pl.CostEstimate(
            flops=2 * slots * blocks * length, bytes_accessed=4 * rows * length, transcendentals=0
        ),
    )(index, count)


STEPS = 16384.0
VMEM = pl.BlockSpec(memory_space=pltpu.VMEM)


def update_kernel(total_ref, table_ref, coded_ref):
    workers = coded_ref.shape[0]
    share, length = total_ref.shape
    update = jnp.dot(
        total_ref[...] * (1.0 / workers),
        table_ref[...],
        precision=lax.Precision.HIGHEST,
        preferred_element_type=jnp.float32,
    )
    largest = jnp.max(jnp.abs(update), axis=0, keepdims=True)
    exponent = jnp.ceil(jnp.log2(jnp.maximum(largest, 1e-30)))
    value = jnp.round(update * (jnp.exp2(-exponent) * STEPS))
    exponent = jnp.broadcast_to(exponent, (coded_ref.shape[1] - share, length))
    rows = jnp.concatenate([value, exponent], axis=0).astype(jnp.int32).astype(jnp.int16)
    for w in range(workers):
        coded_ref[w] = rows


def coded_update(total, table, workers):
    share, length = total.shape
    return pl.pallas_call(
        update_kernel,
        in_specs=[VMEM, VMEM],
        out_specs=VMEM,
        out_shape=jax.ShapeDtypeStruct((workers, share + 8, length), jnp.int16),
    )(total, table)


def decode_kernel(coded_ref, update_ref):
    share = coded_ref.shape[1] - 8
    for w in range(coded_ref.shape[0]):
        first = w * share
        last = min(first + share, update_ref.shape[0])
        if first < last:
            rows = coded_ref[w].astype(jnp.int32).astype(jnp.float32)
            scale = jnp.exp2(rows[share : share + 1]) * (1.0 / STEPS)
            update_ref[first:last] = (rows[:share] * scale)[: last - first]


def decoded(coded, rows):
    return pl.pallas_call(
        decode_kernel,
        in_specs=[VMEM],
        out_specs=VMEM,
        out_shape=jax.ShapeDtypeStruct((rows, coded.shape[2]), jnp.float32),
    )(coded)


def product_kernel(order_ref, *refs):
    pieces, refs = refs[:4], refs[4:]
    weight_ref, gate_ref, up_ref, gate_grad_ref, up_grad_ref, total_ref, act_ref, slope_ref, rows_ref = refs
    step = pl.program_id(0)
    last = pl.num_programs(0) - 1

    @pl.when(step == 0)
    def _():
        gate = gate_ref[...].astype(jnp.float32)
        sigmoid = jax.nn.sigmoid(gate)
        act_ref[...] = gate * sigmoid
        slope_ref[...] = up_ref[...].astype(jnp.float32) * sigmoid * (1.0 + gate * (1.0 - sigmoid))

    for i, piece in enumerate(pieces):
        for j in range(piece.shape[0]):
            rows_ref[order_ref[4 + j], order_ref[i]] = piece[j]
    width = weight_ref.shape[2]
    rows = rows_ref[...].reshape(-1, rows_ref.shape[3])
    total = None
    for b in range(weight_ref.shape[0]):
        term = lax.dot_general(
            weight_ref[b],
            rows[:, b * width : (b + 1) * width],
            (((1,), (1,)), ((), ())),
            preferred_element_type=jnp.float32,
        )
        total = term if total is None else total + term

    @pl.when(step == 0)
    def _():
        total_ref[...] = total

    @pl.when((step > 0) & (step < last))
    def _():
        total_ref[...] += total

    @pl.when(step == last)
    def _():
        hidden_grad = total_ref[...] + total
        up_grad_ref[...] = (hidden_grad * act_ref[...]).astype(jnp.bfloat16)
        gate_grad_ref[...] = (hidden_grad * slope_ref[...]).astype(jnp.bfloat16)


def product(order, pieces, weight, gate, up):
    blocks, rows, width = weight.shape
    tokens = gate.shape[1]
    groups, depth, features = pieces[0].shape
    per_step = blocks // 2
    whole = pl.BlockSpec((rows, tokens), lambda k, order: (0, 0))
    piece = pl.BlockSpec((groups, depth, per_step * width), lambda k, order: (0, 0, k))
    return pl.pallas_call(
        product_kernel,
        grid_spec=pltpu.PrefetchScalarGridSpec(
            num_scalar_prefetch=1,
            grid=(blocks // per_step,),
            in_specs=[piece] * 4
            + [pl.BlockSpec((per_step, rows, width), lambda k, order: (k, 0, 0)), whole, whole],
            out_specs=[whole, whole],
            scratch_shapes=[pltpu.VMEM((rows, tokens), jnp.float32)] * 3
            + [pltpu.VMEM((groups, 4, depth, per_step * width), jnp.bfloat16)],
        ),
        out_shape=[jax.ShapeDtypeStruct((rows, tokens), jnp.bfloat16)] * 2,
        compiler_params=pltpu.CompilerParams(dimension_semantics=("arbitrary",)),
        cost_estimate=pl.CostEstimate(
            flops=2 * rows * tokens * features,
            bytes_accessed=2 * (tokens + rows) * features + 8 * rows * tokens,
            transcendentals=rows * tokens,
        ),
    )(order, *pieces, weight, gate, up)


def per_device_body(out_grad, gate_pre, up_pre, down_weight, momentum, band_index, band_count):
    worker_rows = gate_pre.shape[0]
    own_rows = gate_pre.shape[1]
    window = momentum.shape[2]
    workers = lax.axis_size(DP)
    block_count = band_index.shape[1]
    length = own_rows * window // block_count

    window_grad = gathered(out_grad[:, :window], FSDP).reshape(worker_rows, window)
    weight = lax.all_gather(down_weight, DP)
    own_piece = gathered_over_y(out_grad)
    order = arrival_order()
    pieces = [own_piece]
    for s in SHIFTS[1:]:
        pieces.append(lax.ppermute(own_piece, "x", [(i, (i + s) % 4) for i in range(4)]))

    gate_float = gate_pre.astype(jnp.float32)
    hidden = (gate_float * jax.nn.sigmoid(gate_float) * up_pre.astype(jnp.float32)).astype(
        jnp.bfloat16
    )
    grad_scale = 1.0 / math.sqrt(worker_rows)
    worker_grad = grad_scale * lax.dot_general(
        hidden, window_grad, (((0,), (0,)), ((), ())), preferred_element_type=jnp.float32
    )
    share = -(-block_count // workers)
    share = -(-share // 8) * 8
    rows = share * workers
    mask = band_mask(band_index[0].T, band_count, rows, length)

    cosine_table = jnp.asarray(cosine_matrix(length))
    mixed = momentum_decay * momentum[0] + worker_grad
    spread = jnp.pad(mixed, ((0, rows - block_count), (0, 0)))
    spectrum = jnp.dot(spread, cosine_table.T, precision=lax.Precision.HIGH)
    sent = jnp.where(mask > 0.0, spectrum, 0.0)
    new_momentum = mixed - jnp.dot(sent[:block_count], cosine_table, precision=lax.Precision.HIGH)

    parts = lax.all_to_all(sent.reshape(workers, share, length), DP, 0, 0)
    coded = coded_update(parts.sum(0), cosine_table, workers)
    arrived = lax.all_to_all(coded, DP, 0, 0)
    update = decoded(arrived, block_count)

    gate_grad, up_grad = product(order, pieces, weight, gate_pre.T, up_pre.T)
    return (gate_grad.T, up_grad.T, new_momentum[None], update)


def solution(mesh):
    torus = Mesh(mesh.devices.reshape(8, 2, 8, 4), ("z", "core", "y", "x"))
    both = ("z", "core", "y", "x")
    return jax.shard_map(
        per_device_body,
        mesh=torus,
        in_specs=(
            P(both, None),
            P(DP, FSDP),
            P(DP, FSDP),
            P(FSDP, DP),
            P(DP, FSDP, None),
            P(DP, FSDP, None),
            P(DP, FSDP),
        ),
        out_specs=(P(DP, FSDP), P(DP, FSDP), P(DP, FSDP, None), P(FSDP, None)),
        check_vma=False,
    )
```

```python
import math

import jax
import jax.numpy as jnp
import numpy as np
from jax import lax
from jax.experimental import pallas as pl
from jax.experimental.pallas import tpu as pltpu
from jax.sharding import Mesh
from jax.sharding import PartitionSpec as P


DP = ("z", "core")
FSDP = ("y", "x")
momentum_decay = 0.9
SHIFTS = (0, 1, 3, 2)


def cosine_matrix(length):
    frequency = np.arange(length, dtype=np.float64)[:, None]
    position = np.arange(length, dtype=np.float64)[None, :]
    row_weight = np.where(frequency == 0.0, math.sqrt(1.0 / length), math.sqrt(2.0 / length))
    return (np.cos(math.pi * (position + 0.5) * frequency / length) * row_weight).astype(np.float32)


def gathered(value, axis):
    count = lax.axis_size(axis)
    copies = jnp.broadcast_to(value[None], (count, *value.shape))
    return lax.all_to_all(copies, axis, 0, 0)


def gathered_over_y(value):
    near = lax.ppermute(value, "y", [(i, i ^ 1) for i in range(8)])
    pair = jnp.stack([value, near])
    links = [(i, (i - 1) % 8 if i % 2 == 0 else (i + 1) % 8) for i in range(8)]
    second = lax.ppermute(pair, "y", links)
    four = jnp.concatenate([pair, second])
    links = [(i, (i + 3) % 8 if i % 2 == 0 else (i - 3) % 8) for i in range(8)]
    third = lax.ppermute(four, "y", links)
    return jnp.concatenate([four, third])


def arrival_order():
    def second(y):
        return (y - 1) % 8 if y % 2 == 0 else (y + 1) % 8

    def third(y):
        return (y + 3) % 8 if y % 2 == 0 else (y - 3) % 8

    table = []
    for y in range(8):
        pairs = [y, second(y), third(y), second(third(y))]
        blocks = [b for p in pairs for b in (p, p ^ 1)]
        table += [[(x - s) % 4 for s in SHIFTS] + blocks for x in range(4)]
    row = lax.axis_index("y") * 4 + lax.axis_index("x")
    table = jnp.asarray(np.array(table, np.int32))
    return lax.dynamic_slice(table, (row, 0), (1, table.shape[1]))[0]


def mask_kernel(index_ref, count_ref, mask_ref):
    slots, blocks = index_ref.shape
    length = mask_ref.shape[1]
    index = index_ref[...]
    slot = lax.broadcasted_iota(jnp.int32, (slots, blocks), 0)
    bit = jnp.where(slot < count_ref[...], lax.shift_left(jnp.ones_like(index), index & 31), 0)
    word = lax.shift_right_logical(index, 5)
    place = lax.broadcasted_iota(jnp.int32, (32, blocks), 0)
    parts = []
    for w in range(length // 32):
        value = jnp.sum(jnp.where(word == w, bit, 0), axis=0, keepdims=True)
        ones = lax.shift_right_logical(jnp.broadcast_to(value, place.shape), place) & 1
        parts.append(ones.astype(jnp.float32))
    mask_ref[...] = jnp.zeros_like(mask_ref)
    mask_ref[:blocks] = jnp.concatenate(parts, axis=0).T.astype(mask_ref.dtype)


def band_mask(index, count, rows, length):
    slots, blocks = index.shape
    return pl.pallas_call(
        mask_kernel,
        out_shape=jax.ShapeDtypeStruct((rows, length), jnp.bfloat16),
        cost_estimate=pl.CostEstimate(
            flops=2 * slots * blocks * length, bytes_accessed=4 * rows * length, transcendentals=0
        ),
    )(index, count)


STEPS = 16384.0
VMEM = pl.BlockSpec(memory_space=pltpu.VMEM)


def update_kernel(total_ref, table_ref, coded_ref):
    workers = coded_ref.shape[0]
    share, length = total_ref.shape
    update = jnp.dot(
        total_ref[...] * (1.0 / workers),
        table_ref[...],
        precision=lax.Precision.HIGHEST,
        preferred_element_type=jnp.float32,
    )
    largest = jnp.max(jnp.abs(update), axis=0, keepdims=True)
    exponent = jnp.ceil(jnp.log2(jnp.maximum(largest, 1e-30)))
    value = jnp.round(update * (jnp.exp2(-exponent) * STEPS))
    exponent = jnp.broadcast_to(exponent, (coded_ref.shape[1] - share, length))
    rows = jnp.concatenate([value, exponent], axis=0).astype(jnp.int32).astype(jnp.int16)
    for w in range(workers):
        coded_ref[w] = rows


def coded_update(total, table, workers):
    share, length = total.shape
    return pl.pallas_call(
        update_kernel,
        in_specs=[VMEM, VMEM],
        out_specs=VMEM,
        out_shape=jax.ShapeDtypeStruct((workers, share + 8, length), jnp.int16),
    )(*[pltpu.with_memory_space_constraint(v, pltpu.VMEM) for v in (total, table)])


def decode_kernel(coded_ref, update_ref):
    share = coded_ref.shape[1] - 8
    for w in range(coded_ref.shape[0]):
        first = w * share
        last = min(first + share, update_ref.shape[0])
        if first < last:
            rows = coded_ref[w].astype(jnp.int32).astype(jnp.float32)
            scale = jnp.exp2(rows[share : share + 1]) * (1.0 / STEPS)
            update_ref[first:last] = (rows[:share] * scale)[: last - first]


def decoded(coded, rows):
    return pl.pallas_call(
        decode_kernel,
        in_specs=[VMEM],
        out_specs=VMEM,
        out_shape=jax.ShapeDtypeStruct((rows, coded.shape[2]), jnp.float32),
    )(pltpu.with_memory_space_constraint(coded, pltpu.VMEM))


def product_kernel(order_ref, *refs):
    pieces, refs = refs[:4], refs[4:]
    weight_ref, gate_ref, up_ref, gate_grad_ref, up_grad_ref, total_ref, act_ref, slope_ref, rows_ref = refs
    step = pl.program_id(0)
    last = pl.num_programs(0) - 1

    @pl.when(step == 0)
    def _():
        gate = gate_ref[...].astype(jnp.float32)
        sigmoid = jax.nn.sigmoid(gate)
        act_ref[...] = gate * sigmoid
        slope_ref[...] = up_ref[...].astype(jnp.float32) * sigmoid * (1.0 + gate * (1.0 - sigmoid))

    for i, piece in enumerate(pieces):
        for j in range(piece.shape[0]):
            rows_ref[order_ref[4 + j], order_ref[i]] = piece[j]
    width = weight_ref.shape[2]
    rows = rows_ref[...].reshape(-1, rows_ref.shape[3])
    total = None
    for b in range(weight_ref.shape[0]):
        term = lax.dot_general(
            weight_ref[b],
            rows[:, b * width : (b + 1) * width],
            (((1,), (1,)), ((), ())),
            preferred_element_type=jnp.float32,
        )
        total = term if total is None else total + term

    @pl.when(step == 0)
    def _():
        total_ref[...] = total

    @pl.when((step > 0) & (step < last))
    def _():
        total_ref[...] += total

    @pl.when(step == last)
    def _():
        hidden_grad = total_ref[...] + total
        up_grad_ref[...] = (hidden_grad * act_ref[...]).astype(jnp.bfloat16)
        gate_grad_ref[...] = (hidden_grad * slope_ref[...]).astype(jnp.bfloat16)


def product(order, pieces, weight, gate, up):
    blocks, rows, width = weight.shape
    tokens = gate.shape[1]
    groups, depth, features = pieces[0].shape
    per_step = blocks // 2
    whole = pl.BlockSpec((rows, tokens), lambda k, order: (0, 0))
    piece = pl.BlockSpec((groups, depth, per_step * width), lambda k, order: (0, 0, k))
    return pl.pallas_call(
        product_kernel,
        grid_spec=pltpu.PrefetchScalarGridSpec(
            num_scalar_prefetch=1,
            grid=(blocks // per_step,),
            in_specs=[piece] * 4
            + [pl.BlockSpec((per_step, rows, width), lambda k, order: (k, 0, 0)), whole, whole],
            out_specs=[whole, whole],
            scratch_shapes=[pltpu.VMEM((rows, tokens), jnp.float32)] * 3
            + [pltpu.VMEM((groups, 4, depth, per_step * width), jnp.bfloat16)],
        ),
        out_shape=[jax.ShapeDtypeStruct((rows, tokens), jnp.bfloat16)] * 2,
        compiler_params=pltpu.CompilerParams(dimension_semantics=("arbitrary",)),
        cost_estimate=pl.CostEstimate(
            flops=2 * rows * tokens * features,
            bytes_accessed=2 * (tokens + rows) * features + 8 * rows * tokens,
            transcendentals=rows * tokens,
        ),
    )(order, *pieces, weight, gate, up)


def per_device_body(out_grad, gate_pre, up_pre, down_weight, momentum, band_index, band_count):
    worker_rows = gate_pre.shape[0]
    own_rows = gate_pre.shape[1]
    window = momentum.shape[2]
    workers = lax.axis_size(DP)
    block_count = band_index.shape[1]
    length = own_rows * window // block_count

    window_grad = gathered(out_grad[:, :window], FSDP).reshape(worker_rows, window)
    weight = lax.all_gather(down_weight, DP)
    own_piece = gathered_over_y(out_grad)
    order = arrival_order()
    pieces = [own_piece]
    for s in SHIFTS[1:]:
        pieces.append(lax.ppermute(own_piece, "x", [(i, (i + s) % 4) for i in range(4)]))

    gate_float = gate_pre.astype(jnp.float32)
    hidden = (gate_float * jax.nn.sigmoid(gate_float) * up_pre.astype(jnp.float32)).astype(
        jnp.bfloat16
    )
    hidden = lax.optimization_barrier(hidden)
    grad_scale = 1.0 / math.sqrt(worker_rows)
    worker_grad = grad_scale * lax.dot_general(
        hidden, window_grad, (((0,), (0,)), ((), ())), preferred_element_type=jnp.float32
    )
    share = -(-block_count // workers)
    share = -(-share // 8) * 8
    rows = share * workers
    mask = band_mask(band_index[0].T, band_count, rows, length)

    cosine_table = jnp.asarray(cosine_matrix(length))
    mixed = momentum_decay * momentum[0] + worker_grad
    spread = jnp.pad(mixed, ((0, rows - block_count), (0, 0)))
    spectrum = jnp.dot(spread, cosine_table.T, precision=lax.Precision.HIGH)
    sent = jnp.where(mask > 0.0, spectrum, 0.0)
    new_momentum = mixed - jnp.dot(sent[:block_count], cosine_table, precision=lax.Precision.HIGH)

    parts = lax.all_to_all(sent.reshape(workers, share, length), DP, 0, 0)
    coded = coded_update(parts.sum(0), cosine_table, workers)
    arrived = lax.all_to_all(coded, DP, 0, 0)
    update = decoded(arrived, block_count)

    gate_grad, up_grad = product(order, pieces, weight, gate_pre.T, up_pre.T)
    return (gate_grad.T, up_grad.T, new_momentum[None], update)


def solution(mesh):
    torus = Mesh(mesh.devices.reshape(8, 2, 8, 4), ("z", "core", "y", "x"))
    both = ("z", "core", "y", "x")
    return jax.shard_map(
        per_device_body,
        mesh=torus,
        in_specs=(
            P(both, None),
            P(DP, FSDP),
            P(DP, FSDP),
            P(FSDP, DP),
            P(DP, FSDP, None),
            P(DP, FSDP, None),
            P(DP, FSDP),
        ),
        out_specs=(P(DP, FSDP), P(DP, FSDP), P(DP, FSDP, None), P(FSDP, None)),
        check_vma=False,
    )
```

```python
import math

import jax
import jax.numpy as jnp
import numpy as np
from jax import lax
from jax.experimental import pallas as pl
from jax.experimental.pallas import tpu as pltpu
from jax.sharding import Mesh
from jax.sharding import PartitionSpec as P


DP = ("z", "core")
FSDP = ("y", "x")
momentum_decay = 0.9
VMEM = pl.BlockSpec(memory_space=pltpu.VMEM)
SHIFTS = (0, 1, 3, 2)


def cosine_matrix(length):
    frequency = np.arange(length, dtype=np.float64)[:, None]
    position = np.arange(length, dtype=np.float64)[None, :]
    row_weight = np.where(frequency == 0.0, math.sqrt(1.0 / length), math.sqrt(2.0 / length))
    return (np.cos(math.pi * (position + 0.5) * frequency / length) * row_weight).astype(np.float32)


def gathered(value, axis):
    count = lax.axis_size(axis)
    copies = jnp.broadcast_to(value[None], (count, *value.shape))
    return lax.all_to_all(copies, axis, 0, 0)


def gathered_over_y(value):
    near = lax.ppermute(value, "y", [(i, i ^ 1) for i in range(8)])
    pair = jnp.stack([value, near])
    links = [(i, (i - 1) % 8 if i % 2 == 0 else (i + 1) % 8) for i in range(8)]
    second = lax.ppermute(pair, "y", links)
    four = jnp.concatenate([pair, second])
    links = [(i, (i + 3) % 8 if i % 2 == 0 else (i - 3) % 8) for i in range(8)]
    third = lax.ppermute(four, "y", links)
    return jnp.concatenate([four, third])


def arrival_order():
    def second(y):
        return (y - 1) % 8 if y % 2 == 0 else (y + 1) % 8

    def third(y):
        return (y + 3) % 8 if y % 2 == 0 else (y - 3) % 8

    table = []
    for y in range(8):
        pairs = [y, second(y), third(y), second(third(y))]
        blocks = [b for p in pairs for b in (p, p ^ 1)]
        table += [[(x - s) % 4 for s in SHIFTS] + blocks for x in range(4)]
    row = lax.axis_index("y") * 4 + lax.axis_index("x")
    table = jnp.asarray(np.array(table, np.int32))
    return lax.dynamic_slice(table, (row, 0), (1, table.shape[1]))[0]


def mask_kernel(index_ref, count_ref, mask_ref):
    slots, blocks = index_ref.shape
    length = mask_ref.shape[1]
    index = index_ref[...]
    slot = lax.broadcasted_iota(jnp.int32, (slots, blocks), 0)
    bit = jnp.where(slot < count_ref[...], lax.shift_left(jnp.ones_like(index), index & 31), 0)
    word = lax.shift_right_logical(index, 5)
    place = lax.broadcasted_iota(jnp.int32, (32, blocks), 0)
    parts = []
    for w in range(length // 32):
        value = jnp.sum(jnp.where(word == w, bit, 0), axis=0, keepdims=True)
        ones = lax.shift_right_logical(jnp.broadcast_to(value, place.shape), place) & 1
        parts.append(ones.astype(jnp.float32))
    mask_ref[...] = jnp.zeros_like(mask_ref)
    mask_ref[:blocks] = jnp.concatenate(parts, axis=0).T.astype(mask_ref.dtype)


def band_mask(index, count, rows, length):
    slots, blocks = index.shape
    return pl.pallas_call(
        mask_kernel,
        out_specs=VMEM,
        out_shape=pltpu.VMEM((rows, length), jnp.float32),
        cost_estimate=pl.CostEstimate(
            flops=2 * slots * blocks * length, bytes_accessed=4 * rows * length, transcendentals=0
        ),
    )(index, count)


STEPS = 16384.0


def update_kernel(total_ref, table_ref, coded_ref):
    workers = coded_ref.shape[0]
    share, length = total_ref.shape
    update = jnp.dot(
        total_ref[...] * (1.0 / workers),
        table_ref[...],
        precision=lax.Precision.HIGHEST,
        preferred_element_type=jnp.float32,
    )
    largest = jnp.max(jnp.abs(update), axis=0, keepdims=True)
    exponent = jnp.ceil(jnp.log2(jnp.maximum(largest, 1e-30)))
    value = jnp.round(update * (jnp.exp2(-exponent) * STEPS))
    exponent = jnp.broadcast_to(exponent, (coded_ref.shape[1] - share, length))
    rows = jnp.concatenate([value, exponent], axis=0).astype(jnp.int32).astype(jnp.int16)
    for w in range(workers):
        coded_ref[w] = rows


def coded_update(total, table, workers):
    share, length = total.shape
    return pl.pallas_call(
        update_kernel,
        in_specs=[VMEM, VMEM],
        out_specs=VMEM,
        out_shape=jax.ShapeDtypeStruct((workers, share + 8, length), jnp.int16),
    )(*[pltpu.with_memory_space_constraint(v, pltpu.VMEM) for v in (total, table)])


def decode_kernel(coded_ref, update_ref):
    share = coded_ref.shape[1] - 8
    for w in range(coded_ref.shape[0]):
        first = w * share
        last = min(first + share, update_ref.shape[0])
        if first < last:
            rows = coded_ref[w].astype(jnp.int32).astype(jnp.float32)
            scale = jnp.exp2(rows[share : share + 1]) * (1.0 / STEPS)
            update_ref[first:last] = (rows[:share] * scale)[: last - first]


def decoded(coded, rows):
    return pl.pallas_call(
        decode_kernel,
        in_specs=[VMEM],
        out_specs=VMEM,
        out_shape=jax.ShapeDtypeStruct((rows, coded.shape[2]), jnp.float32),
    )(pltpu.with_memory_space_constraint(coded, pltpu.VMEM))


def product_kernel(order_ref, *refs):
    pieces, refs = refs[:4], refs[4:]
    weight_ref, gate_ref, up_ref, gate_grad_ref, up_grad_ref, total_ref, act_ref, slope_ref, rows_ref = refs
    step = pl.program_id(0)
    last = pl.num_programs(0) - 1

    @pl.when(step == 0)
    def _():
        gate = gate_ref[...].astype(jnp.float32)
        sigmoid = jax.nn.sigmoid(gate)
        act_ref[...] = gate * sigmoid
        slope_ref[...] = up_ref[...].astype(jnp.float32) * sigmoid * (1.0 + gate * (1.0 - sigmoid))

    depth = rows_ref.shape[3]
    columns = pl.ds(pl.multiple_of(step * depth, depth), depth)
    for i, piece in enumerate(pieces):
        for j in range(piece.shape[0]):
            rows_ref[order_ref[4 + j], order_ref[i]] = piece[j, :, columns]
    width = weight_ref.shape[2]
    rows = rows_ref[...].reshape(-1, rows_ref.shape[3])
    total = None
    for b in range(weight_ref.shape[0]):
        term = lax.dot_general(
            weight_ref[b],
            rows[:, b * width : (b + 1) * width],
            (((1,), (1,)), ((), ())),
            preferred_element_type=jnp.float32,
        )
        total = term if total is None else total + term

    @pl.when(step == 0)
    def _():
        total_ref[...] = total

    @pl.when((step > 0) & (step < last))
    def _():
        total_ref[...] += total

    @pl.when(step == last)
    def _():
        hidden_grad = total_ref[...] + total
        up_grad_ref[...] = (hidden_grad * act_ref[...]).astype(jnp.bfloat16)
        gate_grad_ref[...] = (hidden_grad * slope_ref[...]).astype(jnp.bfloat16)


def product(order, pieces, weight, gate, up):
    blocks, rows, width = weight.shape
    tokens = gate.shape[1]
    groups, depth, features = pieces[0].shape
    per_step = blocks // 2
    whole = pl.BlockSpec((rows, tokens), lambda k, order: (0, 0))
    pieces = [pltpu.with_memory_space_constraint(piece, pltpu.VMEM) for piece in pieces]
    return pl.pallas_call(
        product_kernel,
        grid_spec=pltpu.PrefetchScalarGridSpec(
            num_scalar_prefetch=1,
            grid=(blocks // per_step,),
            in_specs=[VMEM] * 4
            + [pl.BlockSpec((per_step, rows, width), lambda k, order: (k, 0, 0)), whole, whole],
            out_specs=[whole, whole],
            scratch_shapes=[pltpu.VMEM((rows, tokens), jnp.float32)] * 3
            + [pltpu.VMEM((groups, 4, depth, per_step * width), jnp.bfloat16)],
        ),
        out_shape=[jax.ShapeDtypeStruct((rows, tokens), jnp.bfloat16)] * 2,
        compiler_params=pltpu.CompilerParams(dimension_semantics=("arbitrary",)),
        cost_estimate=pl.CostEstimate(
            flops=2 * rows * tokens * features,
            bytes_accessed=2 * (tokens + rows) * features + 8 * rows * tokens,
            transcendentals=rows * tokens,
        ),
    )(order, *pieces, weight, gate, up)


def per_device_body(out_grad, gate_pre, up_pre, down_weight, momentum, band_index, band_count):
    worker_rows = gate_pre.shape[0]
    own_rows = gate_pre.shape[1]
    window = momentum.shape[2]
    workers = lax.axis_size(DP)
    block_count = band_index.shape[1]
    length = own_rows * window // block_count

    window_grad = gathered(out_grad[:, :window], FSDP).reshape(worker_rows, window)
    weight = lax.all_gather(down_weight, DP)
    own_piece = gathered_over_y(out_grad)
    order = arrival_order()
    pieces = [own_piece]
    for s in SHIFTS[1:]:
        pieces.append(lax.ppermute(own_piece, "x", [(i, (i + s) % 4) for i in range(4)]))

    gate_float = gate_pre.astype(jnp.float32)
    hidden = (gate_float * jax.nn.sigmoid(gate_float) * up_pre.astype(jnp.float32)).astype(
        jnp.bfloat16
    )
    hidden = lax.optimization_barrier(hidden)
    grad_scale = 1.0 / math.sqrt(worker_rows)
    worker_grad = grad_scale * lax.dot_general(
        hidden, window_grad, (((0,), (0,)), ((), ())), preferred_element_type=jnp.float32
    )
    share = -(-block_count // workers)
    share = -(-share // 8) * 8
    rows = share * workers
    mask = band_mask(band_index[0].T, band_count, rows, length)

    cosine_table = jnp.asarray(cosine_matrix(length))
    mixed = momentum_decay * momentum[0] + worker_grad
    spread = jnp.pad(mixed, ((0, rows - block_count), (0, 0)))
    spectrum = jnp.dot(spread, cosine_table.T, precision=lax.Precision.HIGH)
    sent = jnp.where(mask > 0.0, spectrum, 0.0)
    new_momentum = mixed - jnp.dot(sent[:block_count], cosine_table, precision=lax.Precision.HIGH)

    parts = lax.all_to_all(sent.reshape(workers, share, length), DP, 0, 0)
    coded = coded_update(parts.sum(0), cosine_table, workers)
    arrived = lax.all_to_all(coded, DP, 0, 0)
    update = decoded(arrived, block_count)

    gate_grad, up_grad = product(order, pieces, weight, gate_pre.T, up_pre.T)
    return (gate_grad.T, up_grad.T, new_momentum[None], update)


def solution(mesh):
    torus = Mesh(mesh.devices.reshape(8, 2, 8, 4), ("z", "core", "y", "x"))
    both = ("z", "core", "y", "x")
    return jax.shard_map(
        per_device_body,
        mesh=torus,
        in_specs=(
            P(both, None),
            P(DP, FSDP),
            P(DP, FSDP),
            P(FSDP, DP),
            P(DP, FSDP, None),
            P(DP, FSDP, None),
            P(DP, FSDP),
        ),
        out_specs=(P(DP, FSDP), P(DP, FSDP), P(DP, FSDP, None), P(FSDP, None)),
        check_vma=False,
    )
```

```python
import math

import jax
import jax.numpy as jnp
import numpy as np
from jax import lax
from jax.experimental import pallas as pl
from jax.experimental.pallas import tpu as pltpu
from jax.sharding import Mesh
from jax.sharding import PartitionSpec as P


DP = ("z", "core")
FSDP = ("y", "x")
momentum_decay = 0.9
VMEM = pl.BlockSpec(memory_space=pltpu.VMEM)
SHIFTS = (0, 1, 3, 2)


def cosine_matrix(length):
    frequency = np.arange(length, dtype=np.float64)[:, None]
    position = np.arange(length, dtype=np.float64)[None, :]
    row_weight = np.where(frequency == 0.0, math.sqrt(1.0 / length), math.sqrt(2.0 / length))
    return (np.cos(math.pi * (position + 0.5) * frequency / length) * row_weight).astype(np.float32)


def gathered(value, axis):
    count = lax.axis_size(axis)
    copies = jnp.broadcast_to(value[None], (count, *value.shape))
    return lax.all_to_all(copies, axis, 0, 0)


def gathered_over_y(value):
    near = lax.ppermute(value, "y", [(i, i ^ 1) for i in range(8)])
    pair = jnp.stack([value, near])
    links = [(i, (i - 1) % 8 if i % 2 == 0 else (i + 1) % 8) for i in range(8)]
    second = lax.ppermute(pair, "y", links)
    four = jnp.concatenate([pair, second])
    links = [(i, (i + 3) % 8 if i % 2 == 0 else (i - 3) % 8) for i in range(8)]
    third = lax.ppermute(four, "y", links)
    return jnp.concatenate([four, third])


def arrival_order():
    def second(y):
        return (y - 1) % 8 if y % 2 == 0 else (y + 1) % 8

    def third(y):
        return (y + 3) % 8 if y % 2 == 0 else (y - 3) % 8

    table = []
    for y in range(8):
        pairs = [y, second(y), third(y), second(third(y))]
        blocks = [b for p in pairs for b in (p, p ^ 1)]
        table += [[(x - s) % 4 for s in SHIFTS] + blocks for x in range(4)]
    row = lax.axis_index("y") * 4 + lax.axis_index("x")
    table = jnp.asarray(np.array(table, np.int32))
    return lax.dynamic_slice(table, (row, 0), (1, table.shape[1]))[0]


def mask_kernel(index_ref, count_ref, mask_ref):
    slots, blocks = index_ref.shape
    length = mask_ref.shape[1]
    index = index_ref[...]
    slot = lax.broadcasted_iota(jnp.int32, (slots, blocks), 0)
    bit = jnp.where(slot < count_ref[...], lax.shift_left(jnp.ones_like(index), index & 31), 0)
    word = lax.shift_right_logical(index, 5)
    place = lax.broadcasted_iota(jnp.int32, (32, blocks), 0)
    parts = []
    for w in range(length // 32):
        value = jnp.sum(jnp.where(word == w, bit, 0), axis=0, keepdims=True)
        ones = lax.shift_right_logical(jnp.broadcast_to(value, place.shape), place) & 1
        parts.append(ones.astype(jnp.float32))
    mask_ref[...] = jnp.zeros_like(mask_ref)
    mask_ref[:blocks] = jnp.concatenate(parts, axis=0).T.astype(mask_ref.dtype)


def band_mask(index, count, rows, length):
    slots, blocks = index.shape
    return pl.pallas_call(
        mask_kernel,
        out_specs=VMEM,
        out_shape=pltpu.VMEM((rows, length), jnp.float32),
        cost_estimate=pl.CostEstimate(
            flops=2 * slots * blocks * length, bytes_accessed=4 * rows * length, transcendentals=0
        ),
    )(index, count)


STEPS = 16384.0


def coded_rows(values):
    parts, _, length = values.shape
    largest = jnp.max(jnp.abs(values), axis=1)
    exponent = jnp.ceil(jnp.log2(jnp.maximum(largest, 1e-30)))
    steps = jnp.round(values * (jnp.exp2(-exponent) * STEPS)[:, None, :])
    exponent = jnp.broadcast_to(exponent[:, None, :], (parts, 8, length))
    return jnp.concatenate([steps, exponent], axis=1).astype(jnp.int32).astype(jnp.int16)


def values_of(coded):
    rows = coded.astype(jnp.int32).astype(jnp.float32)
    share = rows.shape[1] - 8
    return rows[:, :share] * (jnp.exp2(rows[:, share : share + 1]) * (1.0 / STEPS))


def spectrum_kernel(mixed_ref, table_ref, mask_ref, coded_ref, sent_ref):
    def split(x):
        high = x.astype(jnp.bfloat16)
        return high, (x - high.astype(jnp.float32)).astype(jnp.bfloat16)

    def dot(x, y):
        return lax.dot_general(
            x, y, (((1,), (1,)), ((), ())), preferred_element_type=jnp.float32
        )

    blocks, length = mixed_ref.shape
    high, low = split(mixed_ref[...])
    table_high, table_low = split(table_ref[...])
    spectrum = dot(high, table_high) + (dot(low, table_high) + dot(high, table_low))
    sent_ref[:blocks] = jnp.where(mask_ref[:blocks] > 0.0, spectrum, 0.0)
    sent_ref[blocks:] = jnp.zeros((sent_ref.shape[0] - blocks, length), jnp.float32)
    workers, height, _ = coded_ref.shape
    coded_ref[...] = coded_rows(sent_ref[...].reshape(workers, height - 8, length))


def coded_spectrum(mixed, table, mask, workers):
    rows, length = mask.shape
    operands = [pltpu.with_memory_space_constraint(v, pltpu.VMEM) for v in (mixed, table, mask)]
    return pl.pallas_call(
        spectrum_kernel,
        in_specs=[VMEM] * 3,
        out_specs=[VMEM, VMEM],
        out_shape=[
            jax.ShapeDtypeStruct((workers, rows // workers + 8, length), jnp.int16),
            jax.ShapeDtypeStruct((rows, length), jnp.float32),
        ],
        cost_estimate=pl.CostEstimate(
            flops=6 * rows * length * length, bytes_accessed=4 * rows * length, transcendentals=0
        ),
    )(*operands)


def update_kernel(parts_ref, table_ref, coded_ref):
    workers = coded_ref.shape[0]
    update = jnp.dot(
        jnp.sum(values_of(parts_ref[...]), axis=0) * (1.0 / workers),
        table_ref[...],
        precision=lax.Precision.HIGHEST,
        preferred_element_type=jnp.float32,
    )
    rows = coded_rows(update[None])[0]
    for w in range(workers):
        coded_ref[w] = rows


def coded_update(parts, table):
    return pl.pallas_call(
        update_kernel,
        in_specs=[VMEM, VMEM],
        out_specs=VMEM,
        out_shape=jax.ShapeDtypeStruct(parts.shape, jnp.int16),
    )(*[pltpu.with_memory_space_constraint(v, pltpu.VMEM) for v in (parts, table)])


def decode_kernel(coded_ref, update_ref):
    share = coded_ref.shape[1] - 8
    for w in range(coded_ref.shape[0]):
        first = w * share
        last = min(first + share, update_ref.shape[0])
        if first < last:
            rows = coded_ref[w].astype(jnp.int32).astype(jnp.float32)
            scale = jnp.exp2(rows[share : share + 1]) * (1.0 / STEPS)
            update_ref[first:last] = (rows[:share] * scale)[: last - first]


def decoded(coded, rows):
    return pl.pallas_call(
        decode_kernel,
        in_specs=[VMEM],
        out_specs=VMEM,
        out_shape=jax.ShapeDtypeStruct((rows, coded.shape[2]), jnp.float32),
    )(pltpu.with_memory_space_constraint(coded, pltpu.VMEM))


def product_kernel(order_ref, *refs):
    pieces, refs = refs[:4], refs[4:]
    weight_ref, gate_ref, up_ref, gate_grad_ref, up_grad_ref, total_ref, act_ref, slope_ref, rows_ref = refs
    step = pl.program_id(0)
    last = pl.num_programs(0) - 1

    @pl.when(step == 0)
    def _():
        gate = gate_ref[...].astype(jnp.float32)
        sigmoid = jax.nn.sigmoid(gate)
        act_ref[...] = gate * sigmoid
        slope_ref[...] = up_ref[...].astype(jnp.float32) * sigmoid * (1.0 + gate * (1.0 - sigmoid))

    depth = rows_ref.shape[3]
    columns = pl.ds(pl.multiple_of(step * depth, depth), depth)
    for i, piece in enumerate(pieces):
        for j in range(piece.shape[0]):
            rows_ref[order_ref[4 + j], order_ref[i]] = piece[j, :, columns]
    width = weight_ref.shape[2]
    rows = rows_ref[...].reshape(-1, rows_ref.shape[3])
    total = None
    for b in range(weight_ref.shape[0]):
        term = lax.dot_general(
            weight_ref[b],
            rows[:, b * width : (b + 1) * width],
            (((1,), (1,)), ((), ())),
            preferred_element_type=jnp.float32,
        )
        total = term if total is None else total + term

    @pl.when(step == 0)
    def _():
        total_ref[...] = total

    @pl.when((step > 0) & (step < last))
    def _():
        total_ref[...] += total

    @pl.when(step == last)
    def _():
        hidden_grad = total_ref[...] + total
        up_grad_ref[...] = (hidden_grad * act_ref[...]).astype(jnp.bfloat16)
        gate_grad_ref[...] = (hidden_grad * slope_ref[...]).astype(jnp.bfloat16)


def product(order, pieces, weight, gate, up):
    blocks, rows, width = weight.shape
    tokens = gate.shape[1]
    groups, depth, features = pieces[0].shape
    per_step = blocks // 2
    whole = pl.BlockSpec((rows, tokens), lambda k, order: (0, 0))
    pieces = [pltpu.with_memory_space_constraint(piece, pltpu.VMEM) for piece in pieces]
    return pl.pallas_call(
        product_kernel,
        grid_spec=pltpu.PrefetchScalarGridSpec(
            num_scalar_prefetch=1,
            grid=(blocks // per_step,),
            in_specs=[VMEM] * 4
            + [pl.BlockSpec((per_step, rows, width), lambda k, order: (k, 0, 0)), whole, whole],
            out_specs=[whole, whole],
            scratch_shapes=[pltpu.VMEM((rows, tokens), jnp.float32)] * 3
            + [pltpu.VMEM((groups, 4, depth, per_step * width), jnp.bfloat16)],
        ),
        out_shape=[jax.ShapeDtypeStruct((rows, tokens), jnp.bfloat16)] * 2,
        compiler_params=pltpu.CompilerParams(dimension_semantics=("arbitrary",)),
        cost_estimate=pl.CostEstimate(
            flops=2 * rows * tokens * features,
            bytes_accessed=2 * (tokens + rows) * features + 8 * rows * tokens,
            transcendentals=rows * tokens,
        ),
    )(order, *pieces, weight, gate, up)


def per_device_body(out_grad, gate_pre, up_pre, down_weight, momentum, band_index, band_count):
    worker_rows = gate_pre.shape[0]
    own_rows = gate_pre.shape[1]
    window = momentum.shape[2]
    workers = lax.axis_size(DP)
    block_count = band_index.shape[1]
    length = own_rows * window // block_count

    window_grad = gathered(out_grad[:, :window], FSDP).reshape(worker_rows, window)
    weight = lax.all_gather(down_weight, DP)
    own_piece = gathered_over_y(out_grad)
    order = arrival_order()
    pieces = [own_piece]
    for s in SHIFTS[1:]:
        pieces.append(lax.ppermute(own_piece, "x", [(i, (i + s) % 4) for i in range(4)]))

    gate_float = gate_pre.astype(jnp.float32)
    hidden = (gate_float * jax.nn.sigmoid(gate_float) * up_pre.astype(jnp.float32)).astype(
        jnp.bfloat16
    )
    hidden = lax.optimization_barrier(hidden)
    grad_scale = 1.0 / math.sqrt(worker_rows)
    worker_grad = grad_scale * lax.dot_general(
        hidden, window_grad, (((0,), (0,)), ((), ())), preferred_element_type=jnp.float32
    )
    share = -(-block_count // workers)
    share = -(-share // 8) * 8
    rows = share * workers
    mask = band_mask(band_index[0].T, band_count, rows, length)

    cosine_table = jnp.asarray(cosine_matrix(length))
    mixed = momentum_decay * momentum[0] + worker_grad
    coded_sent, sent = coded_spectrum(mixed, cosine_table, mask, workers)
    new_momentum = mixed - jnp.dot(sent[:block_count], cosine_table, precision=lax.Precision.HIGH)

    parts = lax.all_to_all(coded_sent, DP, 0, 0)
    coded = coded_update(parts, cosine_table)
    arrived = lax.all_to_all(coded, DP, 0, 0)
    update = decoded(arrived, block_count)

    gate_grad, up_grad = product(order, pieces, weight, gate_pre.T, up_pre.T)
    return (gate_grad.T, up_grad.T, new_momentum[None], update)


def solution(mesh):
    torus = Mesh(mesh.devices.reshape(8, 2, 8, 4), ("z", "core", "y", "x"))
    both = ("z", "core", "y", "x")
    return jax.shard_map(
        per_device_body,
        mesh=torus,
        in_specs=(
            P(both, None),
            P(DP, FSDP),
            P(DP, FSDP),
            P(FSDP, DP),
            P(DP, FSDP, None),
            P(DP, FSDP, None),
            P(DP, FSDP),
        ),
        out_specs=(P(DP, FSDP), P(DP, FSDP), P(DP, FSDP, None), P(FSDP, None)),
        check_vma=False,
    )
```
